256 devices in a mesh: slab: 32 (over y, z), row: 8 (over x, core).
Axes of the slice: x: 4, y: 4, z: 8, core: 2. Of those that a mesh axis runs over, the one named last changes fastest.
Arguments:
- estimate: bfloat16 [3, 256, 4096, 128], P(None, 'row', 'slab'), may hold values from 0.19921875 to 5
- observed: bfloat16 [3, 256, 4096, 128], P(None, 'row', 'slab'), may hold values from 0.099609375 to 10
- interp_table: bfloat16 [16, 128, 128], replicated, may hold values from 0 to 0.75
- psf_taps: float32 [3, 3, 41], replicated, may hold values from 0.001 to 1.32
- background: float32 [3], replicated, may hold values from 0.05 to 0.5
- block_offset: int32 [32, 256, 1], P('slab', 'row'), may hold values from 0 to 4; in each aligned block of 32 rows (0 to 31, 32 to 63, ..., all dimensions but the last counted through in order) at most 16 rows name the same one
- interp_index: int32 [32, 256], P('slab', 'row'), may hold values from 0 to 15
Outputs:
- new_estimate: bfloat16 [3, 256, 4096, 128], P(None, 'row', 'slab')
The draws below stay inside these ranges and needn't reach their ends.
Inputs may be any that keep to these rules, and one draw needn't show every extreme that they name: `block_offset`: among the camera rows of one device no offset is named by more than 16 rows, and some device's rows name one offset exactly 16 times.
All inputs are finite; a program needn't handle non-finite values.
Results may differ from the reference program's by a relative error of at most 0.007.
Values may be sent and summed in bfloat16 or wider, within the bound.
No kernel may reach another device: no remote copies, remote signals or barrier semaphores. Data moves between devices by JAX's collectives and lax.ppermute only.
A program may use at most 128 MiB of HBM per device.

```python
import math
import jax
import jax.numpy as jnp
import numpy as np
from jax import lax

C = 3
BLOCK = 128
HALF = 20
TAPS = 41
NTAB = 16
NY_DEV = 32
COLS = 128
MOST = 16
SPAN = 4
NY = 256
NP = 4096
N_SLAB = 32
N_ROW = 8


def draw_interp_table(key, part):
    band_width = max(2, min(8, BLOCK // 16))
    main_key, side_key = jax.random.split(jax.random.fold_in(key, 11))
    out_index = jnp.arange(BLOCK, dtype=jnp.int32)[:, None]
    in_index = jnp.arange(BLOCK, dtype=jnp.int32)[None, :]
    distance = jnp.abs(in_index - out_index)[None, :, :]
    upper_end = 0.7
    diagonal = jax.random.uniform(main_key, (NTAB, BLOCK, BLOCK), jnp.float32, 0.5, upper_end)
    beside = jax.random.uniform(side_key, (NTAB, BLOCK, BLOCK), jnp.float32, 0.0, 0.24 / band_width)
    matrix = jnp.where(distance == 0, diagonal, jnp.where(distance <= band_width, beside, jnp.float32(0.0)))
    return matrix.astype(jnp.bfloat16)


def draw_psf_taps(key, part):
    peak_key, tail_key = jax.random.split(jax.random.fold_in(key, 23))
    offset_taps = jnp.arange(TAPS, dtype=jnp.float32) - HALF
    peak_low = 0.8
    peak_high = 1.2
    tail_low = 0.002
    tail_high = 0.008
    factor = jax.random.uniform(peak_key, (C, 3, TAPS), jnp.float32, peak_low, peak_high)
    floor_level = jax.random.uniform(tail_key, (C, 3, TAPS), jnp.float32, tail_low, tail_high)
    profile = jnp.exp(-2.0 * offset_taps * offset_taps)[None, None, :]
    return (factor * profile + floor_level).astype(jnp.float32)


def plant(values, key, smallest, top_value):
    dims = values.shape
    index_at = [jax.random.randint(jax.random.fold_in(key, axis), (), 0, dims[axis]) for axis in range(len(dims))]
    values = values.at[tuple(index_at)].set(smallest)
    longest = dims.index(max(dims))
    index_at[longest] = (index_at[longest] + 1) % dims[longest]
    return values.at[tuple(index_at)].set(top_value)


def block_levels(key, dims, cuts, low, high):
    gain, own = 1.0, jax.random.fold_in(key, 6)
    for position, blocks in cuts:
        draws = jnp.exp(jax.random.uniform(jax.random.fold_in(own, position), (blocks,), jnp.float32, low / len(cuts), high / len(cuts)))
        gain = gain * jnp.repeat(draws, dims[position] // blocks).reshape([-1 if axis == position else 1 for axis in range(len(dims))])
    return gain


def routed_block(key, own, number, rows, amount, top, bound, lean):
    order = jax.random.permutation(key, amount)
    packed, usual = portions_of(amount, rows * top, bound, lean, True), portions_of(amount, rows * top, bound, lean, False)
    places = jnp.arange(amount)

    def named(lengths, turn):
        used = int((lengths > 0).sum())
        fixed = max(1, used // 4)
        passed = fixed + (places - fixed + turn * (used - fixed)) % max(1, amount - fixed)
        return jnp.zeros((amount,), jnp.int32).at[order[jnp.where(places < fixed, places, passed)]].set(jnp.asarray(lengths, jnp.int32))

    lengths = jnp.where(number % 4 == 0, named(packed, number // 4), named(usual, number - number // 4 - 1))
    mixed = jax.random.permutation(jax.random.fold_in(own, 3), amount)
    source_of, taker = mixed[0:amount // 2 * 2:2], mixed[1:amount // 2 * 2:2]
    slack = jnp.minimum(lengths[source_of] - 1, bound - lengths[taker]) // 2
    slack = jnp.where((source_of == order[0]) | (taker == order[0]) | (lengths[taker] == 0), 0, jnp.maximum(slack, 0))
    passed = jax.random.randint(jax.random.fold_in(own, 4), (amount // 2,), 0, 1 << 20) % (slack + 1)
    lengths = lengths.at[source_of].add(-passed).at[taker].add(passed)
    members = jnp.searchsorted(jnp.cumsum(lengths), jnp.arange(rows * top), side="right").astype(jnp.int32)
    table = members.reshape(top, rows).T
    table = table[jax.random.permutation(jax.random.fold_in(own, 1), rows)]
    turn = jax.random.randint(jax.random.fold_in(own, 2), (rows, 1), 0, top)
    return jnp.take_along_axis(table, (jnp.arange(top)[None, :] + turn) % top, axis=1)


def portions_of(count, total, reach, slope, full):
    loads = [(1 << 20) // math.isqrt(standing ** slope) + 1 for standing in range(1, count + 1)]
    largest = reach if full else min(reach, max(-(-total // count), total * loads[0] // sum(loads)))
    least = 1 if total - largest >= count - 1 else 0
    given, rest = [largest] + [least] * (count - 1), total - largest - least * (count - 1)
    while rest > 0:
        movable = [i for i in range(1, count) if given[i] < largest] or [i for i in range(1, count) if given[i] < reach]
        mass, left = sum([loads[i] for i in movable]), rest
        for i in movable:
            more = min(reach - given[i], max(1, left * loads[i] // mass), rest)
            given[i] = given[i] + more
            rest = rest - more
    return np.array(given)


def setup_inputs(seed: int = 0) -> dict:
    keys = jax.random.split(jax.random.key(seed), 8)
    estimate = jnp.clip(jnp.exp(math.log(5.0) - 3.2227897 * jax.random.uniform(keys[0], (C, NY, NP, COLS), jnp.float32) ** block_levels(keys[0], (C, NY, NP, COLS), ((1, 8), (2, 32)), -0.2, 0.2)), 0.19921875, 5.0).astype(jnp.bfloat16)
    observed = jnp.clip(jnp.exp(math.log(10.0) - 4.609084 * jax.random.uniform(keys[1], (C, NY, NP, COLS), jnp.float32) ** block_levels(keys[1], (C, NY, NP, COLS), ((1, 8), (2, 32)), -0.2, 0.2)), 0.099609375, 10.0).astype(jnp.bfloat16)
    interp_table = draw_interp_table(jax.random.fold_in(keys[7], 71), 0)
    psf_taps = draw_psf_taps(jax.random.fold_in(keys[7], 71), 0)
    background = jnp.clip(jnp.exp(jax.random.uniform(keys[4], (C,), jnp.float32, math.log(0.05), math.log(0.5))), 0.05, 0.5)
    block_offset_keys = jax.random.split(jax.random.fold_in(keys[5], 1), N_SLAB * NY // NY_DEV)
    block_offset_turns = jax.random.permutation(jax.random.fold_in(keys[5], 3), N_SLAB * NY // NY_DEV)
    block_offset = jax.vmap(lambda own, number: routed_block(jax.random.fold_in(keys[5], 2), own, number, NY_DEV, SPAN + 1, 1, MOST, 2))(block_offset_keys, block_offset_turns).reshape((N_SLAB, NY, 1))
    interp_index = plant(jax.random.randint(keys[6], (N_SLAB, NY), 0, NTAB), jax.random.fold_in(keys[6], 1), 0, NTAB - 1).astype(jnp.int32)
    return dict(estimate=estimate, observed=observed, interp_table=interp_table, psf_taps=psf_taps, background=background, block_offset=block_offset, interp_index=interp_index)


def toeplitz(kernel, rows_out, cols_in, orient, anchor):
    out_index = jnp.arange(rows_out, dtype=jnp.int32)[:, None]
    in_index = jnp.arange(cols_in, dtype=jnp.int32)[None, :]
    tap_index = orient * (in_index - out_index) + anchor
    matches = tap_index[None, :, :] == jnp.arange(kernel.shape[0], dtype=jnp.int32)[:, None, None]
    picked = jnp.where(matches, kernel.astype(jnp.float32)[:, None, None], jnp.float32(0.0))
    return jnp.sum(picked, axis=0).astype(kernel.dtype)


def blocked(values, along, pieces, extent, matrix, periodic):
    moved = jnp.moveaxis(values, along, 0)
    margin = (matrix.shape[1] - extent) // 2
    if periodic:
        padded = jnp.concatenate([moved[-margin:], moved, moved[:margin]], axis=0)
    else:
        filler = jnp.zeros((margin,) + moved.shape[1:], moved.dtype)
        padded = jnp.concatenate([filler, moved, filler], axis=0)
    weights = matrix.astype(jnp.float32)

    def one_block(index):
        window = lax.dynamic_slice_in_dim(padded, index * extent, extent + 2 * margin, 0)
        return jnp.einsum("e...,qe->q...", window.astype(jnp.float32), weights)

    result = lax.map(one_block, jnp.arange(pieces, dtype=jnp.int32))
    result = result.reshape((pieces * extent,) + moved.shape[1:])
    return jnp.moveaxis(result, 0, along)


def reference(estimate, observed, interp_table, psf_taps, background, block_offset, interp_index):
    rows_all = jnp.arange(NY, dtype=jnp.int32)
    slabs_all = jnp.arange(N_SLAB, dtype=jnp.int32)

    def shear_channel(values):
        blocks = values.reshape(NY, N_SLAB, BLOCK, COLS)

        def add_slab(total, slab):
            chosen = jnp.take(interp_table, interp_index[slab], axis=0).astype(jnp.float32)
            source = lax.dynamic_index_in_dim(blocks, slab, 1, keepdims=False).astype(jnp.float32)
            term = jnp.einsum("yqp,ypx->yqx", chosen, source).astype(jnp.bfloat16)
            owner = ((slab + block_offset[slab, :, 0]) % N_SLAB).astype(jnp.int32)
            total = total.at[rows_all, owner].add(term.astype(jnp.float32))
            return total, None

        start = jnp.zeros((NY, N_SLAB, BLOCK, COLS), jnp.float32)
        total, _ = lax.scan(add_slab, start, slabs_all)
        return total.astype(jnp.bfloat16).reshape(NY, NP, COLS)

    def unshear_channel(values):
        blocks = values.reshape(NY, N_SLAB, BLOCK, COLS)

        def one_slab(slab):
            chosen = jnp.take(interp_table, interp_index[slab], axis=0).astype(jnp.float32)
            owner = ((slab + block_offset[slab, :, 0]) % N_SLAB).astype(jnp.int32)
            landed = blocks[rows_all, owner].astype(jnp.float32)
            return jnp.einsum("yqp,yqx->ypx", chosen, landed)

        parts = lax.map(one_slab, slabs_all)
        return jnp.moveaxis(parts, 0, 1).reshape(NY, NP, COLS)

    def channel(inputs):
        skewed, measured, taps, level = inputs
        kernel = (taps / jnp.sum(taps, axis=1, keepdims=True)).astype(jnp.bfloat16)
        plane_fwd = toeplitz(kernel[0], BLOCK, BLOCK + 2 * HALF, 1, 0)
        plane_adj = toeplitz(kernel[0], BLOCK, BLOCK + 2 * HALF, -1, 2 * HALF)
        row_fwd = toeplitz(kernel[1], NY_DEV, NY_DEV + 2 * HALF, 1, 0)
        row_adj = toeplitz(kernel[1], NY_DEV, NY_DEV + 2 * HALF, -1, 2 * HALF)
        col_fwd = toeplitz(kernel[2], COLS, COLS, 1, HALF).astype(jnp.float32)
        col_adj = toeplitz(kernel[2], COLS, COLS, -1, HALF).astype(jnp.float32)
        sheared = shear_channel(skewed)
        plane_pass = blocked(sheared, 1, N_SLAB, BLOCK, plane_fwd, True).astype(jnp.bfloat16)
        row_pass = blocked(plane_pass, 0, N_ROW, NY_DEV, row_fwd, False).astype(jnp.bfloat16)
        blurred = jnp.einsum("yqx,zx->yqz", row_pass.astype(jnp.float32), col_fwd)
        quotient = (measured.astype(jnp.float32) / (blurred + level)).astype(jnp.bfloat16)
        column_back = jnp.einsum("yqx,zx->yqz", quotient.astype(jnp.float32), col_adj).astype(jnp.bfloat16)
        row_back = blocked(column_back, 0, N_ROW, NY_DEV, row_adj, False).astype(jnp.bfloat16)
        backward = blocked(row_back, 1, N_SLAB, BLOCK, plane_adj, True).astype(jnp.bfloat16)
        correction = unshear_channel(backward)
        return (skewed.astype(jnp.float32) * correction).astype(jnp.bfloat16)

    return lax.map(channel, (estimate, observed, psf_taps, background))
```

```python
import functools

import jax
import jax.numpy as jnp
from jax import lax
from jax.experimental import pallas as pl
from jax.experimental.pallas import tpu as pltpu
from jax.sharding import PartitionSpec as P

HALF = 20
TAPS = 41
RING = 8
LANES = 128
CHUNK = 16
ROW_GROUP = 16
F32 = jnp.float32
BF16 = jnp.bfloat16
PARAMS = pltpu.CompilerParams(vmem_limit_bytes=56 * 1024 * 1024)


def dot_nn(left, right):
    return lax.dot_general(left, right, (((1,), (0,)), ((), ())), preferred_element_type=F32)


def dot_nt(left, right):
    return lax.dot_general(left, right, (((1,), (1,)), ((), ())), preferred_element_type=F32)


def whole(shape):
    return pl.BlockSpec(shape, lambda *_: (0,) * len(shape))


def smem():
    return pl.BlockSpec(memory_space=pltpu.SMEM)


def shape_of(*dims):
    return jax.ShapeDtypeStruct(dims, BF16)


def prepare_body(index_ref, est_ref, obs_ref, table_ref, col_ref, eye_ref, *outs):
    rows = est_ref.shape[1]
    first = pl.program_id(0) * rows
    terms = [
        dot_nn(table_ref[index_ref[first + r]], est_ref[0, r]).astype(BF16) for r in range(rows)
    ]
    turned = dot_nt(col_ref[...], jnp.concatenate(terms, axis=0)).astype(BF16)
    seen = dot_nt(eye_ref[...], obs_ref[0].reshape(rows * LANES, LANES)).astype(BF16)
    for r in range(rows):
        for d in range(RING):
            outs[d][0, r] = turned[d * CHUNK : (d + 1) * CHUNK, r * LANES : (r + 1) * LANES]
            outs[d][1, r] = seen[d * CHUNK : (d + 1) * CHUNK, r * LANES : (r + 1) * LANES]


def prepare(channel, index, estimate, observed, table, col, eye):
    rows = estimate.shape[1]
    step = 8
    volume = pl.BlockSpec((1, step, LANES, LANES), lambda i: (channel, i, 0, 0))
    return pl.pallas_call(
        prepare_body,
        grid=(rows // step,),
        in_specs=[
            smem(),
            volume,
            volume,
            whole(table.shape),
            pl.BlockSpec((None, LANES, LANES), lambda i: (channel, 0, 0)),
            whole(eye.shape),
        ],
        out_specs=[pl.BlockSpec((2, step, CHUNK, LANES), lambda i: (0, i, 0, 0))] * RING,
        out_shape=[shape_of(2, rows, CHUNK, LANES)] * RING,
        compiler_params=PARAMS,
    )(index, estimate, observed, table, col, eye)


def route_body(place_ref, offset_ref, *refs):
    terms = refs[:RING]
    own_ref, up_ref, down_ref, total_ref = refs[RING:]
    rows = own_ref.shape[0]
    total_ref[...] = jnp.zeros(total_ref.shape, F32)
    place = place_ref[0]

    def one_row(row, carry):
        for d in range(RING):
            slab = lax.rem(place + (RING - d), RING)
            slot = slab + offset_ref[slab, row]
            lanes = pl.ds(pl.multiple_of(slot * LANES, LANES), LANES)
            total_ref[row, :, lanes] += terms[d][0, row].astype(F32)
        return carry

    lax.fori_loop(0, rows, one_row, 0)
    own_ref[...] = total_ref[:, :, : RING * LANES].astype(BF16)
    up_ref[:, :, : 4 * LANES] = total_ref[:, :, RING * LANES :].astype(BF16)
    up_ref[:, :, 4 * LANES :] = total_ref[:, :, (RING - 1) * LANES : RING * LANES].astype(BF16)
    down_ref[...] = total_ref[:, :, :LANES].astype(BF16)


def route(place, offsets, parts):
    rows = parts[0].shape[1]
    return pl.pallas_call(
        route_body,
        grid=(1,),
        in_specs=[smem(), smem()] + [whole((1, rows, CHUNK, LANES))] * RING,
        out_specs=[
            whole((rows, CHUNK, RING * LANES)),
            whole((rows, CHUNK, 5 * LANES)),
            whole((rows, CHUNK, LANES)),
        ],
        out_shape=[
            shape_of(rows, CHUNK, RING * LANES),
            shape_of(rows, CHUNK, 5 * LANES),
            shape_of(rows, CHUNK, LANES),
        ],
        scratch_shapes=[pltpu.VMEM((rows, CHUNK, 12 * LANES), F32)],
        compiler_params=PARAMS,
    )(place, offsets, *parts)


def planes_body(own_ref, spill_ref, up_ref, down_ref, matrix_ref, pass_ref, low_ref, high_ref, x_ref):
    rows = own_ref.shape[0]
    x_ref[:, :, :LANES] = up_ref[:, :, 4 * LANES :]
    x_ref[:, :, LANES : 5 * LANES] = (
        own_ref[:, :, : 4 * LANES].astype(F32) + up_ref[:, :, : 4 * LANES].astype(F32)
    ).astype(BF16)
    x_ref[:, :, 5 * LANES : 9 * LANES] = own_ref[:, :, 4 * LANES :]
    x_ref[:, :, 9 * LANES :] = (spill_ref[...].astype(F32) + down_ref[...].astype(F32)).astype(BF16)
    for pair in range(RING // 2):
        at = 2 * LANES * pair
        window = x_ref[:, :, at : at + 4 * LANES].reshape(rows * CHUNK, 4 * LANES)
        result = dot_nn(window, matrix_ref[...]).astype(BF16).reshape(rows, CHUNK, 2 * LANES)
        pass_ref[:, :, at : at + 2 * LANES] = result
        low_ref[:, :, at : at + 2 * LANES] = result[:HALF]
        high_ref[:, :, at : at + 2 * LANES] = result[rows - HALF :]


def planes(channel, own, sent_up, from_below, from_above, matrix):
    rows = own.shape[0]
    full, edge = (rows, CHUNK, RING * LANES), (HALF, CHUNK, RING * LANES)
    return pl.pallas_call(
        planes_body,
        grid=(1,),
        in_specs=[
            whole(full),
            whole((rows, CHUNK, LANES)),
            whole((rows, CHUNK, 5 * LANES)),
            whole((rows, CHUNK, LANES)),
            pl.BlockSpec((None, 4 * LANES, 2 * LANES), lambda i: (channel, 0, 0)),
        ],
        out_specs=[whole(full), whole(edge), whole(edge)],
        out_shape=[shape_of(*full), shape_of(*edge), shape_of(*edge)],
        scratch_shapes=[pltpu.VMEM((rows, CHUNK, 10 * LANES), BF16)],
        compiler_params=PARAMS,
    )(own, sent_up, from_below, from_above, matrix)


def joined_rows(x_ref, low_ref, own_ref, high_ref):
    rows = own_ref.shape[0]
    x_ref[:HALF] = low_ref[...]
    x_ref[HALF : HALF + rows] = own_ref[...]
    x_ref[HALF + rows :] = high_ref[...]


def row_sums(x_ref, matrix_ref, group):
    window = x_ref[group * ROW_GROUP : (group + 1) * ROW_GROUP + 2 * HALF]
    flat = window.reshape((ROW_GROUP + 2 * HALF) * CHUNK, RING * LANES)
    return dot_nn(matrix_ref[...], flat).reshape(ROW_GROUP, CHUNK, RING * LANES)


def quotient_body(place_ref, level_ref, own_ref, low_ref, high_ref, matrix_ref, *refs):
    seen = refs[:RING]
    quot_ref, to_low_ref, to_high_ref, x_ref, obs_ref = refs[RING:]
    rows = own_ref.shape[0]
    joined_rows(x_ref, low_ref, own_ref, high_ref)
    for d in range(RING):
        slab = lax.rem(place_ref[0] + (RING - d), RING)
        obs_ref[:, :, pl.ds(pl.multiple_of(slab * LANES, LANES), LANES)] = seen[d][0]
    for group in range(rows // ROW_GROUP):
        at = group * ROW_GROUP
        blurred = row_sums(x_ref, matrix_ref, group)
        quot_ref[at : at + ROW_GROUP] = (
            obs_ref[at : at + ROW_GROUP].astype(F32) / (blurred + level_ref[0])
        ).astype(BF16)
    to_low_ref[...] = quot_ref[:HALF]
    to_high_ref[...] = quot_ref[rows - HALF :]


def quotient(channel, place, level, own, low, high, matrix, parts):
    rows = own.shape[0]
    full, edge = (rows, CHUNK, RING * LANES), (HALF, CHUNK, RING * LANES)
    seen = pl.BlockSpec((1, rows, CHUNK, LANES), lambda i: (1, 0, 0, 0))
    return pl.pallas_call(
        quotient_body,
        grid=(1,),
        in_specs=[
            smem(),
            smem(),
            whole(full),
            whole(edge),
            whole(edge),
            pl.BlockSpec((None,) + matrix.shape[1:], lambda i: (channel, 0, 0)),
        ]
        + [seen] * RING,
        out_specs=[whole(full), whole(edge), whole(edge)],
        out_shape=[shape_of(*full), shape_of(*edge), shape_of(*edge)],
        scratch_shapes=[
            pltpu.VMEM((rows + 2 * HALF, CHUNK, RING * LANES), BF16),
            pltpu.VMEM(full, BF16),
        ],
        compiler_params=PARAMS,
    )(place, level, own, low, high, matrix, *parts)


def rows_back_body(own_ref, low_ref, high_ref, matrix_ref, back_ref, down_ref, up_ref, x_ref):
    rows = own_ref.shape[0]
    joined_rows(x_ref, low_ref, own_ref, high_ref)
    for group in range(rows // ROW_GROUP):
        at = group * ROW_GROUP
        result = row_sums(x_ref, matrix_ref, group).astype(BF16)
        back_ref[at : at + ROW_GROUP] = result
        down_ref[at : at + ROW_GROUP] = result[:, :, : 5 * LANES]
        up_ref[at : at + ROW_GROUP] = result[:, :, (RING - 1) * LANES :]


def rows_back(channel, own, low, high, matrix):
    rows = own.shape[0]
    full, edge = (rows, CHUNK, RING * LANES), (HALF, CHUNK, RING * LANES)
    return pl.pallas_call(
        rows_back_body,
        grid=(1,),
        in_specs=[
            whole(full),
            whole(edge),
            whole(edge),
            pl.BlockSpec((None,) + matrix.shape[1:], lambda i: (channel, 0, 0)),
        ],
        out_specs=[
            whole(full),
            whole((rows, CHUNK, 5 * LANES)),
            whole((rows, CHUNK, LANES)),
        ],
        out_shape=[
            shape_of(*full),
            shape_of(rows, CHUNK, 5 * LANES),
            shape_of(rows, CHUNK, LANES),
        ],
        scratch_shapes=[pltpu.VMEM((rows + 2 * HALF, CHUNK, RING * LANES), BF16)],
        compiler_params=PARAMS,
    )(own, low, high, matrix)


def collect_body(place_ref, offset_ref, own_ref, above_ref, below_ref, matrix_ref, *refs):
    outs = refs[:RING]
    x_ref, back_ref = refs[RING:]
    rows = own_ref.shape[0]
    x_ref[:, :, :LANES] = below_ref[...]
    x_ref[:, :, LANES : 9 * LANES] = own_ref[...]
    x_ref[:, :, 9 * LANES :] = above_ref[...]
    for pair in range(6):
        at = 2 * LANES * pair
        window = x_ref[:, :, at : at + 4 * LANES].reshape(rows * CHUNK, 4 * LANES)
        result = dot_nn(window, matrix_ref[...]).astype(BF16).reshape(rows, CHUNK, 2 * LANES)
        back_ref[:, :, at : at + 2 * LANES] = result
    place = place_ref[0]

    def one_row(row, carry):
        for d in range(RING):
            slab = lax.rem(place + d, RING)
            slot = slab + offset_ref[slab, row]
            outs[d][row] = back_ref[row, :, pl.ds(pl.multiple_of(slot * LANES, LANES), LANES)]
        return carry

    lax.fori_loop(0, rows, one_row, 0)


def collect(channel, place, offsets, own, above, below, matrix):
    rows = own.shape[0]
    return pl.pallas_call(
        collect_body,
        grid=(1,),
        in_specs=[
            smem(),
            smem(),
            whole(own.shape),
            whole(above.shape),
            whole(below.shape),
            pl.BlockSpec((None, 4 * LANES, 2 * LANES), lambda i: (channel, 0, 0)),
        ],
        out_specs=[whole((rows, CHUNK, LANES))] * RING,
        out_shape=[shape_of(rows, CHUNK, LANES)] * RING,
        scratch_shapes=[
            pltpu.VMEM((rows, CHUNK, 14 * LANES), BF16),
            pltpu.VMEM((rows, CHUNK, 12 * LANES), BF16),
        ],
        compiler_params=PARAMS,
    )(place, offsets, own, above, below, matrix)


def update_body(index_ref, est_ref, turned_ref, col_ref, *refs):
    parts, out_ref = refs[:RING], refs[RING]
    rows = est_ref.shape[1]
    first = pl.program_id(0) * rows
    for r in range(rows):
        block = jnp.concatenate([parts[d][r] for d in range(RING)], axis=0)
        back = dot_nn(col_ref[...], block).astype(BF16)
        correction = dot_nt(turned_ref[index_ref[first + r]], back)
        out_ref[r] = (est_ref[0, r].astype(F32) * correction).astype(BF16)


def update(channel, index, estimate, turned, col, parts):
    rows = estimate.shape[1]
    step = 8
    return pl.pallas_call(
        update_body,
        grid=(rows // step,),
        in_specs=[
            smem(),
            pl.BlockSpec((1, step, LANES, LANES), lambda i: (channel, i, 0, 0)),
            whole(turned.shape),
            pl.BlockSpec((None, LANES, LANES), lambda i: (channel, 0, 0)),
        ]
        + [pl.BlockSpec((step, CHUNK, LANES), lambda i: (i, 0, 0))] * RING,
        out_specs=pl.BlockSpec((step, LANES, LANES), lambda i: (i, 0, 0)),
        out_shape=shape_of(rows, LANES, LANES),
        compiler_params=PARAMS,
    )(index, estimate, turned, col, *parts)


def banded(kernel, tap_index):
    matches = (
        tap_index[None, :, :] == jnp.arange(TAPS, dtype=jnp.int32)[:, None, None]
    ).astype(BF16)
    return jnp.einsum("ct,tab->cab", kernel, matches, preferred_element_type=F32).astype(BF16)


def iotas(first, second):
    return (
        jnp.arange(first, dtype=jnp.int32)[:, None],
        jnp.arange(second, dtype=jnp.int32)[None, :],
    )


def row_matrix(kernel, back):
    width = ROW_GROUP + 2 * HALF
    out, taken = iotas(ROW_GROUP, width)
    small = banded(kernel, out - taken + 2 * HALF if back else taken - out)
    wide_out, wide_in = iotas(ROW_GROUP * CHUNK, width * CHUNK)
    left = (wide_out // CHUNK == jnp.arange(ROW_GROUP, dtype=jnp.int32)[None, :]).astype(BF16)
    right = (jnp.arange(width, dtype=jnp.int32)[:, None] == wide_in // CHUNK).astype(BF16)
    spread = jnp.einsum("ao,cow->caw", left, small, preferred_element_type=F32).astype(BF16)
    spread = jnp.einsum("caw,wb->cab", spread, right, preferred_element_type=F32)
    same = wide_out % CHUNK == wide_in % CHUNK
    return jnp.where(same[None], spread, F32(0.0)).astype(BF16)


def shifted(array, axis, pairs):
    return lax.ppermute(array, axis, pairs)


def per_device(estimate, observed, interp_table, psf_taps, background, block_offset, interp_index):
    channels = estimate.shape[0]
    slabs = lax.axis_size("slab")
    groups = slabs // RING
    lines = lax.axis_size("row")
    ring = [
        [(g * RING + z, g * RING + (z + d) % RING) for g in range(groups) for z in range(RING)]
        for d in range(RING)
    ]
    up = [(i, (i + RING) % slabs) for i in range(slabs)]
    down = [(i, (i - RING) % slabs) for i in range(slabs)]
    right = [(i, i + 1) for i in range(lines - 1)]
    left = [(i + 1, i) for i in range(lines - 1)]
    far_first = [4, 3, 5, 2, 6, 1, 7]

    place = lax.rem(lax.axis_index("slab"), RING).astype(jnp.int32)
    spot = place[None]
    index = interp_index[0]
    offsets = lax.all_gather(
        block_offset[0, :, 0],
        "slab",
        axis_index_groups=[[g * RING + z for z in range(RING)] for g in range(groups)],
    )
    kernel = (psf_taps / jnp.sum(psf_taps, axis=2, keepdims=True)).astype(BF16)
    wide_out, wide_in = iotas(LANES, LANES)
    sent = (wide_out + place * CHUNK) % LANES
    col_fwd = banded(kernel[:, 2], wide_in - sent + HALF)
    eye = (sent == wide_in).astype(BF16)
    got = (CHUNK * (place - wide_in // CHUNK)) % LANES + wide_in % CHUNK
    col_adj = banded(kernel[:, 2], wide_out - got + HALF)
    taken, out = iotas(4 * LANES, 2 * LANES)
    plane_fwd = banded(kernel[:, 0], taken - out - LANES + HALF)
    plane_adj = banded(kernel[:, 0], out - taken + LANES + HALF)
    row_fwd = row_matrix(kernel[:, 1], False)
    row_adj = row_matrix(kernel[:, 1], True)
    turned_table = jnp.swapaxes(interp_table, 1, 2)

    def spread_ring(parts):
        moved = {d: shifted(parts[d], "slab", ring[d]) for d in far_first}
        return [parts[0]] + [moved[d] for d in range(1, RING)]

    arrived = []
    for c in range(channels):
        arrived.append(
            spread_ring(prepare(c, index, estimate, observed, interp_table, col_fwd, eye))
        )
    results = []
    for c in range(channels):
        parts = arrived[c]
        own, to_up, to_down = route(spot, offsets, parts)
        from_below = shifted(to_up, "slab", up)
        from_above = shifted(to_down, "slab", down)
        passed, to_low, to_high = planes(c, own, to_up, from_below, from_above, plane_fwd)
        low = shifted(to_high, "row", right)
        high = shifted(to_low, "row", left)
        quot, to_low, to_high = quotient(
            c, spot, background[c : c + 1], passed, low, high, row_fwd, parts
        )
        low = shifted(to_high, "row", right)
        high = shifted(to_low, "row", left)
        back, to_down, to_up = rows_back(c, quot, low, high, row_adj)
        from_above = shifted(to_down, "slab", down)
        from_below = shifted(to_up, "slab", up)
        parts = collect(c, spot, offsets, back, from_above, from_below, plane_adj)
        parts = spread_ring(parts)
        results.append(update(c, index, estimate, turned_table, col_adj, parts))
    return jnp.stack(results)


def solution(mesh):
    in_specs = (
        P(None, "row", "slab", None),
        P(None, "row", "slab", None),
        P(),
        P(),
        P(),
        P("slab", "row", None),
        P("slab", "row"),
    )
    out_specs = P(None, "row", "slab", None)
    return jax.shard_map(
        per_device, mesh=mesh, in_specs=in_specs, out_specs=out_specs, check_vma=False
    )
```

```python
import functools

import jax
import jax.numpy as jnp
from jax import lax
from jax.experimental import pallas as pl
from jax.experimental.pallas import tpu as pltpu
from jax.sharding import PartitionSpec as P

HALF = 20
TAPS = 41
RING = 8
LANES = 128
CHUNK = 16
ROW_GROUP = 16
F32 = jnp.float32
BF16 = jnp.bfloat16
PARAMS = pltpu.CompilerParams(vmem_limit_bytes=56 * 1024 * 1024)


def dot_nn(left, right):
    return lax.dot_general(left, right, (((1,), (0,)), ((), ())), preferred_element_type=F32)


def dot_nt(left, right):
    return lax.dot_general(left, right, (((1,), (1,)), ((), ())), preferred_element_type=F32)


def whole(shape):
    return pl.BlockSpec(shape, lambda *_: (0,) * len(shape))


def smem():
    return pl.BlockSpec(memory_space=pltpu.SMEM)


def shape_of(*dims):
    return jax.ShapeDtypeStruct(dims, BF16)


def launch(body, operands, in_specs, after=(), **rest):
    count = len(operands)

    def run(*refs):
        body(*refs[:count], *refs[count + len(after) :])

    return pl.pallas_call(
        run,
        in_specs=[*in_specs] + [pl.BlockSpec(memory_space=pl.ANY)] * len(after),
        compiler_params=PARAMS,
        **rest,
    )(*operands, *after)


def tap_rows(taps_ref, width, place_of):
    taps = taps_ref[...]
    kernel = (taps / jnp.sum(taps, axis=1, keepdims=True)).astype(BF16)
    tap = lax.broadcasted_iota(jnp.int32, (TAPS, width), 0)
    lane = lax.broadcasted_iota(jnp.int32, (TAPS, width), 1)
    return dot_nn(kernel, (lane == place_of(tap)).astype(BF16))


def slanted(row, height):
    spread = jnp.broadcast_to(row, (height, row.shape[1]))
    return pltpu.roll(spread, 0, 1, stride=1, stride_axis=0)


def column_weights_body(place_ref, taps_ref, fwd_ref, adj_ref, eye_ref):
    width = 2 * LANES
    fwd = tap_rows(taps_ref, width, lambda t: (t - HALF) & (width - 1))
    adj = tap_rows(taps_ref, width, lambda t: (HALF - t) & (width - 1))
    first = place_ref[0] * CHUNK
    for c in range(fwd_ref.shape[0]):
        at = 3 * c + 2
        square = slanted(fwd[at : at + 1], LANES)[:, :LANES]
        turned = pltpu.roll(square, lax.rem(LANES - first, LANES), 0)
        fwd_ref[c] = turned.astype(BF16)
        adj_ref[c] = slanted(adj[at : at + 1], LANES)[:, :LANES].astype(BF16)
    out = lax.broadcasted_iota(jnp.int32, (LANES, LANES), 0)
    taken = lax.broadcasted_iota(jnp.int32, (LANES, LANES), 1)
    eye_ref[...] = (((out + first) & (LANES - 1)) == taken).astype(BF16)


def column_weights(place, taps, channels):
    square = shape_of(channels, LANES, LANES)
    return pl.pallas_call(
        column_weights_body,
        grid=(1,),
        in_specs=[smem(), whole(taps.shape)],
        out_specs=[whole(square.shape), whole(square.shape), whole((LANES, LANES))],
        out_shape=[square, square, shape_of(LANES, LANES)],
        compiler_params=PARAMS,
    )(place, taps)


PLANE_WIDTH = 6 * LANES
ROW_WIDTH = 9 * LANES
WINDOW = (ROW_GROUP + 2 * HALF) * CHUNK


def band_weights_body(taps_ref, plane_fwd_ref, plane_adj_ref, row_fwd_ref, row_adj_ref):
    start = PLANE_WIDTH - LANES - HALF
    plane_fwd = tap_rows(taps_ref, PLANE_WIDTH, lambda t: start + 2 * HALF - t)
    plane_adj = tap_rows(taps_ref, PLANE_WIDTH, lambda t: start + t)
    row_fwd = tap_rows(taps_ref, ROW_WIDTH, lambda t: CHUNK * t)
    row_adj = tap_rows(taps_ref, ROW_WIDTH, lambda t: CHUNK * (2 * HALF - t))
    for c in range(plane_fwd_ref.shape[0]):
        plane, row = slice(3 * c, 3 * c + 1), slice(3 * c + 1, 3 * c + 2)
        for ref, band in ((plane_fwd_ref, plane_fwd), (plane_adj_ref, plane_adj)):
            ref[c] = slanted(band[plane], 4 * LANES)[:, : 2 * LANES].astype(BF16)
        for ref, band in ((row_fwd_ref, row_fwd), (row_adj_ref, row_adj)):
            ref[c] = slanted(band[row], ROW_GROUP * CHUNK)[:, :WINDOW].astype(BF16)


def band_weights(taps, channels):
    plane = shape_of(channels, 4 * LANES, 2 * LANES)
    row = shape_of(channels, ROW_GROUP * CHUNK, WINDOW)
    return pl.pallas_call(
        band_weights_body,
        grid=(1,),
        in_specs=[whole(taps.shape)],
        out_specs=[whole(v.shape) for v in (plane, plane, row, row)],
        out_shape=[plane, plane, row, row],
        compiler_params=PARAMS,
    )(taps)


STEP = 8


def send_terms_body(index_ref, est_ref, table_ref, col_ref, offset_ref, *outs):
    step = pl.program_id(0)
    blocks = pl.num_programs(0) - 1
    per_channel = LANES // CHUNK * 4 // STEP

    @pl.when(step < blocks)
    def _():
        first = lax.rem(step, per_channel) * STEP
        terms = [
            dot_nn(table_ref[index_ref[first + r]], est_ref[0, r]).astype(BF16)
            for r in range(STEP)
        ]
        turned = dot_nt(col_ref[0], jnp.concatenate(terms, axis=0)).astype(BF16)
        for r in range(STEP):
            for d in range(RING):
                outs[d][r] = turned[d * CHUNK : (d + 1) * CHUNK, r * LANES : (r + 1) * LANES]

    @pl.when(step == blocks)
    def _():
        for d in range(RING):
            outs[d][0] = offset_ref[...]


def send_terms(index, estimate, table, col, offset_tile):
    channels, rows = estimate.shape[:2]
    per_channel = rows // STEP
    blocks = channels * per_channel
    size = channels * rows + 1

    def at(i):
        j = jnp.minimum(i, blocks - 1)
        return j // per_channel, j % per_channel

    return pl.pallas_call(
        send_terms_body,
        grid=(blocks + 1,),
        in_specs=[
            smem(),
            pl.BlockSpec((1, STEP, LANES, LANES), lambda i: (*at(i), 0, 0)),
            whole(table.shape),
            pl.BlockSpec((1, LANES, LANES), lambda i: (at(i)[0], 0, 0)),
            whole(offset_tile.shape),
        ],
        out_specs=[pl.BlockSpec((STEP, CHUNK, LANES), lambda i: (i, 0, 0))] * RING,
        out_shape=[shape_of(size, CHUNK, LANES)] * RING,
        compiler_params=PARAMS,
    )(index, estimate, table, col, offset_tile)


def send_observed_body(obs_ref, eye_ref, after_ref, *outs):
    seen = dot_nt(eye_ref[...], obs_ref[0].reshape(STEP * LANES, LANES)).astype(BF16)
    for r in range(STEP):
        for d in range(RING):
            outs[d][r] = seen[d * CHUNK : (d + 1) * CHUNK, r * LANES : (r + 1) * LANES]


def send_observed(observed, eye, after):
    channels, rows = observed.shape[:2]
    per_channel = rows // STEP
    return pl.pallas_call(
        send_observed_body,
        grid=(channels * per_channel,),
        in_specs=[
            pl.BlockSpec(
                (1, STEP, LANES, LANES), lambda i: (i // per_channel, i % per_channel, 0, 0)
            ),
            whole(eye.shape),
            pl.BlockSpec(memory_space=pl.ANY),
        ],
        out_specs=[pl.BlockSpec((STEP, CHUNK, LANES), lambda i: (i, 0, 0))] * RING,
        out_shape=[shape_of(channels * rows, CHUNK, LANES)] * RING,
        compiler_params=PARAMS,
    )(observed, eye, after)


def route_body(place_ref, offset_ref, *refs):
    terms = refs[:RING]
    own_ref, up_ref, down_ref, total_ref = refs[RING:]
    rows = own_ref.shape[1]
    total_ref[...] = jnp.zeros(total_ref.shape, F32)
    place = place_ref[0]

    def one_row(row, carry):
        for d in range(RING):
            slot = lax.rem(place + (RING - d), RING) + offset_ref[d, row]
            lanes = pl.ds(pl.multiple_of(slot * LANES, LANES), LANES)
            total_ref[row, :, lanes] += terms[d][row].astype(F32)
        return carry

    lax.fori_loop(0, rows, one_row, 0)
    own_ref[0] = total_ref[:, :, : RING * LANES].astype(BF16)
    up_ref[0, :, :, : 4 * LANES] = total_ref[:, :, RING * LANES :].astype(BF16)
    up_ref[0, :, :, 4 * LANES :] = total_ref[:, :, (RING - 1) * LANES : RING * LANES].astype(BF16)
    down_ref[0] = total_ref[:, :, :LANES].astype(BF16)


def each(first, *dims):
    return pl.BlockSpec((1,) + dims, lambda i: (first + i,) + (0,) * len(dims))


def route(channel, rows, place, offsets, parts, after):
    outs = [(rows, CHUNK, RING * LANES), (rows, CHUNK, 5 * LANES), (rows, CHUNK, LANES)]
    return launch(
        route_body,
        [place, offsets, *parts],
        [smem(), smem()] + [pl.BlockSpec((rows, CHUNK, LANES), lambda i: (channel, 0, 0))] * RING,
        after,
        grid=(1,),
        out_specs=[each(0, *dims) for dims in outs],
        out_shape=[shape_of(1, *dims) for dims in outs],
        scratch_shapes=[pltpu.VMEM((rows, CHUNK, 12 * LANES), F32)],
    )


def planes_body(own_ref, spill_ref, up_ref, down_ref, matrix_ref, pass_ref, low_ref, high_ref, x_ref):
    rows = own_ref.shape[1]
    x_ref[:, :, :LANES] = up_ref[0, :, :, 4 * LANES :]
    x_ref[:, :, LANES : 5 * LANES] = (
        own_ref[0, :, :, : 4 * LANES].astype(F32) + up_ref[0, :, :, : 4 * LANES].astype(F32)
    ).astype(BF16)
    x_ref[:, :, 5 * LANES : 9 * LANES] = own_ref[0, :, :, 4 * LANES :]
    x_ref[:, :, 9 * LANES :] = (spill_ref[0].astype(F32) + down_ref[0].astype(F32)).astype(BF16)
    for pair in range(RING // 2):
        at = 2 * LANES * pair
        window = x_ref[:, :, at : at + 4 * LANES].reshape(rows * CHUNK, 4 * LANES)
        result = dot_nn(window, matrix_ref[0]).astype(BF16).reshape(rows, CHUNK, 2 * LANES)
        pass_ref[0, :, :, at : at + 2 * LANES] = result
        low_ref[0, :, :, at : at + 2 * LANES] = result[:HALF]
        high_ref[0, :, :, at : at + 2 * LANES] = result[rows - HALF :]


def planes(first, own, sent_up, from_below, from_above, matrix, after):
    count, rows = own.shape[:2]
    full, edge = (rows, CHUNK, RING * LANES), (HALF, CHUNK, RING * LANES)
    return launch(
        planes_body,
        [own, sent_up, from_below, from_above, matrix],
        [
            each(0, *full),
            each(0, rows, CHUNK, LANES),
            each(0, rows, CHUNK, 5 * LANES),
            each(0, rows, CHUNK, LANES),
            each(first, 4 * LANES, 2 * LANES),
        ],
        after,
        grid=(count,),
        out_specs=[each(0, *full), each(0, *edge), each(0, *edge)],
        out_shape=[shape_of(count, *full), shape_of(count, *edge), shape_of(count, *edge)],
        scratch_shapes=[pltpu.VMEM((rows, CHUNK, 10 * LANES), BF16)],
    )


def joined_rows(x_ref, low_ref, own_ref, high_ref):
    rows = own_ref.shape[1]
    x_ref[:HALF] = low_ref[0]
    x_ref[HALF : HALF + rows] = own_ref[0]
    x_ref[HALF + rows :] = high_ref[0]


def row_sums(x_ref, matrix_ref, group):
    window = x_ref[group * ROW_GROUP : (group + 1) * ROW_GROUP + 2 * HALF]
    flat = window.reshape((ROW_GROUP + 2 * HALF) * CHUNK, RING * LANES)
    return dot_nn(matrix_ref[0], flat).reshape(ROW_GROUP, CHUNK, RING * LANES)


def quotient_body(first, place_ref, level_ref, own_ref, low_ref, high_ref, matrix_ref, *refs):
    seen = refs[:RING]
    quot_ref, to_low_ref, to_high_ref, x_ref, obs_ref = refs[RING:]
    rows = own_ref.shape[1]
    joined_rows(x_ref, low_ref, own_ref, high_ref)
    for d in range(RING):
        slab = lax.rem(place_ref[0] + (RING - d), RING)
        obs_ref[:, :, pl.ds(pl.multiple_of(slab * LANES, LANES), LANES)] = seen[d][...]
    level = level_ref[first + pl.program_id(0)]
    for group in range(rows // ROW_GROUP):
        at = group * ROW_GROUP
        blurred = row_sums(x_ref, matrix_ref, group)
        quot_ref[0, at : at + ROW_GROUP] = (
            obs_ref[at : at + ROW_GROUP].astype(F32) / (blurred + level)
        ).astype(BF16)
    to_low_ref[0] = quot_ref[0, :HALF]
    to_high_ref[0] = quot_ref[0, rows - HALF :]


def quotient(first, place, level, own, low, high, matrix, parts, after):
    count, rows = own.shape[:2]
    full, edge = (rows, CHUNK, RING * LANES), (HALF, CHUNK, RING * LANES)
    return launch(
        functools.partial(quotient_body, first),
        [place, level, own, low, high, matrix, *parts],
        [
            smem(),
            smem(),
            each(0, *full),
            each(0, *edge),
            each(0, *edge),
            each(first, *matrix.shape[1:]),
        ]
        + [pl.BlockSpec((rows, CHUNK, LANES), lambda i: (first, 0, 0))] * RING,
        after,
        grid=(count,),
        out_specs=[each(0, *full), each(0, *edge), each(0, *edge)],
        out_shape=[shape_of(count, *full), shape_of(count, *edge), shape_of(count, *edge)],
        scratch_shapes=[
            pltpu.VMEM((rows + 2 * HALF, CHUNK, RING * LANES), BF16),
            pltpu.VMEM(full, BF16),
        ],
    )


def rows_back_body(own_ref, low_ref, high_ref, matrix_ref, back_ref, down_ref, up_ref, x_ref):
    rows = own_ref.shape[1]
    joined_rows(x_ref, low_ref, own_ref, high_ref)
    for group in range(rows // ROW_GROUP):
        at = group * ROW_GROUP
        result = row_sums(x_ref, matrix_ref, group).astype(BF16)
        back_ref[0, at : at + ROW_GROUP] = result
        down_ref[0, at : at + ROW_GROUP] = result[:, :, : 5 * LANES]
        up_ref[0, at : at + ROW_GROUP] = result[:, :, (RING - 1) * LANES :]


def rows_back(first, own, low, high, matrix, after):
    count, rows = own.shape[:2]
    full, edge = (rows, CHUNK, RING * LANES), (HALF, CHUNK, RING * LANES)
    outs = [full, (rows, CHUNK, 5 * LANES), (rows, CHUNK, LANES)]
    return launch(
        rows_back_body,
        [own, low, high, matrix],
        [
            each(0, *full),
            each(0, *edge),
            each(0, *edge),
            each(first, *matrix.shape[1:]),
        ],
        after,
        grid=(count,),
        out_specs=[each(0, *dims) for dims in outs],
        out_shape=[shape_of(count, *dims) for dims in outs],
        scratch_shapes=[pltpu.VMEM((rows + 2 * HALF, CHUNK, RING * LANES), BF16)],
    )


def collect_body(place_ref, offset_ref, own_ref, above_ref, below_ref, matrix_ref, *refs):
    outs = refs[:RING]
    x_ref, back_ref = refs[RING:]
    rows = own_ref.shape[1]
    x_ref[:, :, :LANES] = below_ref[0]
    x_ref[:, :, LANES : 9 * LANES] = own_ref[0]
    x_ref[:, :, 9 * LANES :] = above_ref[0]
    for pair in range(6):
        at = 2 * LANES * pair
        window = x_ref[:, :, at : at + 4 * LANES].reshape(rows * CHUNK, 4 * LANES)
        result = dot_nn(window, matrix_ref[0]).astype(BF16).reshape(rows, CHUNK, 2 * LANES)
        back_ref[:, :, at : at + 2 * LANES] = result
    place = place_ref[0]

    def one_row(row, carry):
        for d in range(RING):
            slot = lax.rem(place + d, RING) + offset_ref[(RING - d) % RING, row]
            lanes = pl.ds(pl.multiple_of(slot * LANES, LANES), LANES)
            outs[d][0, row] = back_ref[row, :, lanes]
        return carry

    lax.fori_loop(0, rows, one_row, 0)


def collect(first, place, offsets, own, above, below, matrix, after):
    count, rows = own.shape[:2]
    return launch(
        collect_body,
        [place, offsets, own, above, below, matrix],
        [
            smem(),
            smem(),
            each(0, *own.shape[1:]),
            each(0, *above.shape[1:]),
            each(0, *below.shape[1:]),
            each(first, 4 * LANES, 2 * LANES),
        ],
        after,
        grid=(count,),
        out_specs=[each(0, rows, CHUNK, LANES)] * RING,
        out_shape=[shape_of(count, rows, CHUNK, LANES)] * RING,
        scratch_shapes=[
            pltpu.VMEM((rows, CHUNK, 14 * LANES), BF16),
            pltpu.VMEM((rows, CHUNK, 12 * LANES), BF16),
        ],
    )


def update_body(place_ref, index_ref, est_ref, turned_ref, col_ref, *refs):
    parts, out_ref, block_ref = refs[:RING], refs[-2], refs[-1]
    first = pl.program_id(1) * STEP
    for d in range(RING):
        at = CHUNK * lax.rem(place_ref[0] + (RING - d), RING)
        block_ref[:, pl.ds(pl.multiple_of(at, CHUNK), CHUNK)] = parts[d][0]
    for r in range(STEP):
        back = dot_nn(col_ref[0], block_ref[r]).astype(BF16)
        correction = dot_nt(turned_ref[index_ref[first + r]], back)
        out_ref[0, r] = (est_ref[0, r].astype(F32) * correction).astype(BF16)


def update(first, place, index, estimate, turned, col, parts, before):
    rows = estimate.shape[1]
    count = parts[0].shape[0]
    volume = pl.BlockSpec((1, STEP, LANES, LANES), lambda c, i: (first + c, i, 0, 0))
    in_specs = [
        smem(),
        smem(),
        volume,
        whole(turned.shape),
        pl.BlockSpec((1, LANES, LANES), lambda c, i: (first + c, 0, 0)),
    ] + [pl.BlockSpec((1, STEP, CHUNK, LANES), lambda c, i: (c, i, 0, 0))] * RING
    operands = [place, index, estimate, turned, col, *parts]
    aliases = {}
    if before is not None:
        aliases = {len(operands): 0}
        operands.append(before)
        in_specs.append(pl.BlockSpec(memory_space=pl.ANY))
    return pl.pallas_call(
        update_body,
        grid=(count, rows // STEP),
        in_specs=in_specs,
        out_specs=volume,
        out_shape=shape_of(*estimate.shape),
        scratch_shapes=[pltpu.VMEM((STEP, LANES, LANES), BF16)],
        input_output_aliases=aliases,
        compiler_params=PARAMS,
    )(*operands)


def shifted(array, axis, pairs):
    return lax.ppermute(array, axis, pairs)


def per_device(estimate, observed, interp_table, psf_taps, background, block_offset, interp_index):
    channels = estimate.shape[0]
    slabs = lax.axis_size("slab")
    groups = slabs // RING
    lines = lax.axis_size("row")
    ring = [
        [(g * RING + z, g * RING + (z + d) % RING) for g in range(groups) for z in range(RING)]
        for d in range(RING)
    ]
    up = [(i, (i + RING) % slabs) for i in range(slabs)]
    down = [(i, (i - RING) % slabs) for i in range(slabs)]
    right = [(i, i + 1) for i in range(lines - 1)]
    left = [(i + 1, i) for i in range(lines - 1)]
    far_first = [4, 3, 5, 2, 6, 1, 7]

    place = lax.rem(lax.axis_index("slab"), RING).astype(jnp.int32)
    spot = place[None]
    index = interp_index[0]
    rows = estimate.shape[1]
    offset_row = jnp.pad(block_offset[0, :, 0].astype(BF16), (0, LANES - rows))
    offset_tile = jnp.broadcast_to(offset_row[None], (CHUNK, LANES))
    taps = psf_taps.reshape(3 * channels, TAPS)
    col_fwd, col_adj, eye = column_weights(spot, taps, channels)
    turned_table = jnp.swapaxes(interp_table, 1, 2)

    def spread_ring(parts):
        moved = {d: shifted(parts[d], "slab", ring[d]) for d in far_first}
        return [parts[0]] + [moved[d] for d in range(1, RING)]

    plane_fwd, plane_adj, row_fwd, row_adj = band_weights(taps, channels)
    sent = send_terms(index, estimate, interp_table, col_fwd, offset_tile)
    terms = spread_ring(sent)
    sent = send_observed(observed, eye, sent[0])
    seen = spread_ring(sent)
    ready = (sent[0],)
    offsets = jnp.stack([part[channels * rows, 0, :rows] for part in terms]).astype(jnp.int32)

    result, earlier = None, [(), ready, (), (), ()]
    for c in range(channels):
        own, to_up, to_down = route(c, rows, spot, offsets, terms, earlier[1])
        from_below = shifted(to_up, "slab", up)
        from_above = shifted(to_down, "slab", down)
        passed, to_low, to_high = planes(
            c, own, to_up, from_below, from_above, plane_fwd, earlier[2]
        )
        done = [(), (passed,)]
        low = shifted(to_high, "row", right)
        high = shifted(to_low, "row", left)
        quot, to_low, to_high = quotient(
            c, spot, background, passed, low, high, row_fwd, seen, earlier[3]
        )
        done.append((quot,))
        low = shifted(to_high, "row", right)
        high = shifted(to_low, "row", left)
        back, to_down, to_up = rows_back(c, quot, low, high, row_adj, earlier[4])
        done.append((back,))
        from_above = shifted(to_down, "slab", down)
        from_below = shifted(to_up, "slab", up)
        parts = collect(c, spot, offsets, back, from_above, from_below, plane_adj, ())
        done.append((parts[0],))
        parts = spread_ring(parts)
        result = update(c, spot, index, estimate, turned_table, col_adj, parts, result)
        if c == 1:
            done[4] += first_result
        first_result = (result,)
        earlier = done
    return result


def solution(mesh):
    in_specs = (
        P(None, "row", "slab", None),
        P(None, "row", "slab", None),
        P(),
        P(),
        P(),
        P("slab", "row", None),
        P("slab", "row"),
    )
    out_specs = P(None, "row", "slab", None)
    return jax.shard_map(
        per_device, mesh=mesh, in_specs=in_specs, out_specs=out_specs, check_vma=False
    )
```

```python
import functools

import jax
import jax.numpy as jnp
from jax import lax
from jax.experimental import pallas as pl
from jax.experimental.pallas import tpu as pltpu
from jax.sharding import PartitionSpec as P

HALF = 20
TAPS = 41
RING = 8
LANES = 128
CHUNK = 16
ROW_GROUP = 16
F32 = jnp.float32
BF16 = jnp.bfloat16
PARAMS = pltpu.CompilerParams(vmem_limit_bytes=56 * 1024 * 1024)


def dot_nn(left, right):
    return lax.dot_general(left, right, (((1,), (0,)), ((), ())), preferred_element_type=F32)


def dot_nt(left, right):
    return lax.dot_general(left, right, (((1,), (1,)), ((), ())), preferred_element_type=F32)


def whole(shape):
    return pl.BlockSpec(shape, lambda *_: (0,) * len(shape))


def smem():
    return pl.BlockSpec(memory_space=pltpu.SMEM)


def shape_of(*dims):
    return jax.ShapeDtypeStruct(dims, BF16)


def launch(body, operands, in_specs, after=(), **rest):
    count = len(operands)

    def run(*refs):
        body(*refs[:count], *refs[count + len(after) :])

    return pl.pallas_call(
        run,
        in_specs=[*in_specs] + [pl.BlockSpec(memory_space=pl.ANY)] * len(after),
        compiler_params=PARAMS,
        **rest,
    )(*operands, *after)


def tap_rows(taps_ref, width, place_of):
    taps = taps_ref[...]
    kernel = (taps / jnp.sum(taps, axis=1, keepdims=True)).astype(BF16)
    tap = lax.broadcasted_iota(jnp.int32, (TAPS, width), 0)
    lane = lax.broadcasted_iota(jnp.int32, (TAPS, width), 1)
    return dot_nn(kernel, (lane == place_of(tap)).astype(BF16))


def slanted(row, height):
    spread = jnp.broadcast_to(row, (height, row.shape[1]))
    return pltpu.roll(spread, 0, 1, stride=1, stride_axis=0)


def column_weights_body(place_ref, taps_ref, fwd_ref, adj_ref, eye_ref):
    width = 2 * LANES
    fwd = tap_rows(taps_ref, width, lambda t: (t - HALF) & (width - 1))
    adj = tap_rows(taps_ref, width, lambda t: (HALF - t) & (width - 1))
    first = place_ref[0] * CHUNK
    for c in range(fwd_ref.shape[0]):
        at = 3 * c + 2
        square = slanted(fwd[at : at + 1], LANES)[:, :LANES]
        turned = pltpu.roll(square, lax.rem(LANES - first, LANES), 0)
        fwd_ref[c] = turned.astype(BF16)
        adj_ref[c] = slanted(adj[at : at + 1], LANES)[:, :LANES].astype(BF16)
    out = lax.broadcasted_iota(jnp.int32, (LANES, LANES), 0)
    taken = lax.broadcasted_iota(jnp.int32, (LANES, LANES), 1)
    eye_ref[...] = (((out + first) & (LANES - 1)) == taken).astype(BF16)


def column_weights(place, taps, channels):
    square = shape_of(channels, LANES, LANES)
    return pl.pallas_call(
        column_weights_body,
        grid=(1,),
        in_specs=[smem(), whole(taps.shape)],
        out_specs=[whole(square.shape), whole(square.shape), whole((LANES, LANES))],
        out_shape=[square, square, shape_of(LANES, LANES)],
        compiler_params=PARAMS,
    )(place, taps)


PLANE_WIDTH = 6 * LANES
ROW_WIDTH = 9 * LANES
WINDOW = (ROW_GROUP + 2 * HALF) * CHUNK


def band_weights_body(taps_ref, plane_fwd_ref, plane_adj_ref, row_fwd_ref, row_adj_ref):
    start = PLANE_WIDTH - LANES - HALF
    plane_fwd = tap_rows(taps_ref, PLANE_WIDTH, lambda t: start + 2 * HALF - t)
    plane_adj = tap_rows(taps_ref, PLANE_WIDTH, lambda t: start + t)
    row_fwd = tap_rows(taps_ref, ROW_WIDTH, lambda t: CHUNK * t)
    row_adj = tap_rows(taps_ref, ROW_WIDTH, lambda t: CHUNK * (2 * HALF - t))
    for c in range(plane_fwd_ref.shape[0]):
        plane, row = slice(3 * c, 3 * c + 1), slice(3 * c + 1, 3 * c + 2)
        for ref, band in ((plane_fwd_ref, plane_fwd), (plane_adj_ref, plane_adj)):
            ref[c] = slanted(band[plane], 4 * LANES)[:, : 2 * LANES].astype(BF16)
        for ref, band in ((row_fwd_ref, row_fwd), (row_adj_ref, row_adj)):
            ref[c] = slanted(band[row], ROW_GROUP * CHUNK)[:, :WINDOW].astype(BF16)


def band_weights(taps, channels):
    plane = shape_of(channels, 4 * LANES, 2 * LANES)
    row = shape_of(channels, ROW_GROUP * CHUNK, WINDOW)
    return pl.pallas_call(
        band_weights_body,
        grid=(1,),
        in_specs=[whole(taps.shape)],
        out_specs=[whole(v.shape) for v in (plane, plane, row, row)],
        out_shape=[plane, plane, row, row],
        compiler_params=PARAMS,
    )(taps)


STEP = 8


def send_terms_body(index_ref, est_ref, table_ref, col_ref, offset_ref, *outs):
    step = pl.program_id(0)
    blocks = pl.num_programs(0) - 1
    per_channel = LANES // CHUNK * 4 // STEP

    @pl.when(step < blocks)
    def _():
        first = lax.rem(step, per_channel) * STEP
        terms = [
            dot_nn(table_ref[index_ref[first + r]], est_ref[0, r]).astype(BF16)
            for r in range(STEP)
        ]
        turned = dot_nt(col_ref[0], jnp.concatenate(terms, axis=0)).astype(BF16)
        for r in range(STEP):
            for d in range(RING):
                outs[d][r] = turned[d * CHUNK : (d + 1) * CHUNK, r * LANES : (r + 1) * LANES]

    @pl.when(step == blocks)
    def _():
        for d in range(RING):
            outs[d][0] = offset_ref[...]


def send_terms(index, estimate, table, col, offset_tile):
    channels, rows = estimate.shape[:2]
    per_channel = rows // STEP
    blocks = channels * per_channel
    size = channels * rows + 1

    def at(i):
        j = jnp.minimum(i, blocks - 1)
        return j // per_channel, j % per_channel

    return pl.pallas_call(
        send_terms_body,
        grid=(blocks + 1,),
        in_specs=[
            smem(),
            pl.BlockSpec((1, STEP, LANES, LANES), lambda i: (*at(i), 0, 0)),
            whole(table.shape),
            pl.BlockSpec((1, LANES, LANES), lambda i: (at(i)[0], 0, 0)),
            whole(offset_tile.shape),
        ],
        out_specs=[pl.BlockSpec((STEP, CHUNK, LANES), lambda i: (i, 0, 0))] * RING,
        out_shape=[shape_of(size, CHUNK, LANES)] * RING,
        compiler_params=PARAMS,
    )(index, estimate, table, col, offset_tile)


def send_observed_body(obs_ref, eye_ref, after_ref, *outs):
    seen = dot_nt(eye_ref[...], obs_ref[0].reshape(STEP * LANES, LANES)).astype(BF16)
    for r in range(STEP):
        for d in range(RING):
            outs[d][r] = seen[d * CHUNK : (d + 1) * CHUNK, r * LANES : (r + 1) * LANES]


def send_observed(observed, eye, after):
    channels, rows = observed.shape[:2]
    per_channel = rows // STEP
    return pl.pallas_call(
        send_observed_body,
        grid=(channels * per_channel,),
        in_specs=[
            pl.BlockSpec(
                (1, STEP, LANES, LANES), lambda i: (i // per_channel, i % per_channel, 0, 0)
            ),
            whole(eye.shape),
            pl.BlockSpec(memory_space=pl.ANY),
        ],
        out_specs=[pl.BlockSpec((STEP, CHUNK, LANES), lambda i: (i, 0, 0))] * RING,
        out_shape=[shape_of(channels * rows, CHUNK, LANES)] * RING,
        compiler_params=PARAMS,
    )(observed, eye, after)


def route_body(place_ref, offset_ref, *refs):
    terms = refs[:RING]
    own_ref, up_ref, down_ref, total_ref = refs[RING:]
    rows = own_ref.shape[1]
    total_ref[...] = jnp.zeros(total_ref.shape, F32)
    place = place_ref[0]

    def one_row(row, carry):
        for d in range(RING):
            slot = lax.rem(place + (RING - d), RING) + offset_ref[d, row]
            lanes = pl.ds(pl.multiple_of(slot * LANES, LANES), LANES)
            total_ref[row, :, lanes] += terms[d][row].astype(F32)
        return carry

    lax.fori_loop(0, rows, one_row, 0)
    own_ref[0] = total_ref[:, :, : RING * LANES].astype(BF16)
    up_ref[0, :, :, : 4 * LANES] = total_ref[:, :, RING * LANES :].astype(BF16)
    up_ref[0, :, :, 4 * LANES :] = total_ref[:, :, (RING - 1) * LANES : RING * LANES].astype(BF16)
    down_ref[0] = total_ref[:, :, :LANES].astype(BF16)


def each(first, *dims):
    return pl.BlockSpec((1,) + dims, lambda i: (first + i,) + (0,) * len(dims))


def route(channel, rows, place, offsets, parts, after):
    outs = [(rows, CHUNK, RING * LANES), (rows, CHUNK, 5 * LANES), (rows, CHUNK, LANES)]
    return launch(
        route_body,
        [place, offsets, *parts],
        [smem(), smem()] + [pl.BlockSpec((rows, CHUNK, LANES), lambda i: (channel, 0, 0))] * RING,
        after,
        grid=(1,),
        out_specs=[each(0, *dims) for dims in outs],
        out_shape=[shape_of(1, *dims) for dims in outs],
        scratch_shapes=[pltpu.VMEM((rows, CHUNK, 12 * LANES), F32)],
    )


def planes_body(own_ref, spill_ref, up_ref, down_ref, matrix_ref, pass_ref, low_ref, high_ref, x_ref):
    rows = own_ref.shape[1]
    x_ref[:, :, :LANES] = up_ref[0, :, :, 4 * LANES :]
    x_ref[:, :, LANES : 5 * LANES] = (
        own_ref[0, :, :, : 4 * LANES].astype(F32) + up_ref[0, :, :, : 4 * LANES].astype(F32)
    ).astype(BF16)
    x_ref[:, :, 5 * LANES : 9 * LANES] = own_ref[0, :, :, 4 * LANES :]
    x_ref[:, :, 9 * LANES :] = (spill_ref[0].astype(F32) + down_ref[0].astype(F32)).astype(BF16)
    for pair in range(RING // 2):
        at = 2 * LANES * pair
        window = x_ref[:, :, at : at + 4 * LANES].reshape(rows * CHUNK, 4 * LANES)
        result = dot_nn(window, matrix_ref[0]).astype(BF16).reshape(rows, CHUNK, 2 * LANES)
        pass_ref[0, :, :, at : at + 2 * LANES] = result
        low_ref[0, :, :, at : at + 2 * LANES] = result[:HALF]
        high_ref[0, :, :, at : at + 2 * LANES] = result[rows - HALF :]


def planes(first, own, sent_up, from_below, from_above, matrix, after):
    count, rows = own.shape[:2]
    full, edge = (rows, CHUNK, RING * LANES), (HALF, CHUNK, RING * LANES)
    return launch(
        planes_body,
        [own, sent_up, from_below, from_above, matrix],
        [
            each(0, *full),
            each(0, rows, CHUNK, LANES),
            each(0, rows, CHUNK, 5 * LANES),
            each(0, rows, CHUNK, LANES),
            each(first, 4 * LANES, 2 * LANES),
        ],
        after,
        grid=(count,),
        out_specs=[each(0, *full), each(0, *edge), each(0, *edge)],
        out_shape=[shape_of(count, *full), shape_of(count, *edge), shape_of(count, *edge)],
        scratch_shapes=[pltpu.VMEM((rows, CHUNK, 10 * LANES), BF16)],
    )


def joined_rows(x_ref, low_ref, own_ref, high_ref):
    rows = own_ref.shape[1]
    x_ref[:HALF] = low_ref[0]
    x_ref[HALF : HALF + rows] = own_ref[0]
    x_ref[HALF + rows :] = high_ref[0]


def row_sums(x_ref, matrix_ref, group):
    window = x_ref[group * ROW_GROUP : (group + 1) * ROW_GROUP + 2 * HALF]
    flat = window.reshape((ROW_GROUP + 2 * HALF) * CHUNK, RING * LANES)
    return dot_nn(matrix_ref[0], flat).reshape(ROW_GROUP, CHUNK, RING * LANES)


def quotient_body(first, place_ref, level_ref, own_ref, low_ref, high_ref, matrix_ref, *refs):
    seen = refs[:RING]
    quot_ref, to_low_ref, to_high_ref, x_ref, obs_ref = refs[RING:]
    rows = own_ref.shape[1]
    joined_rows(x_ref, low_ref, own_ref, high_ref)
    for d in range(RING):
        slab = lax.rem(place_ref[0] + (RING - d), RING)
        obs_ref[:, :, pl.ds(pl.multiple_of(slab * LANES, LANES), LANES)] = seen[d][...]
    level = level_ref[first + pl.program_id(0)]
    for group in range(rows // ROW_GROUP):
        at = group * ROW_GROUP
        blurred = row_sums(x_ref, matrix_ref, group)
        quot_ref[0, at : at + ROW_GROUP] = (
            obs_ref[at : at + ROW_GROUP].astype(F32) / (blurred + level)
        ).astype(BF16)
    to_low_ref[0] = quot_ref[0, :HALF]
    to_high_ref[0] = quot_ref[0, rows - HALF :]


def quotient(first, place, level, own, low, high, matrix, parts, after):
    count, rows = own.shape[:2]
    full, edge = (rows, CHUNK, RING * LANES), (HALF, CHUNK, RING * LANES)
    return launch(
        functools.partial(quotient_body, first),
        [place, level, own, low, high, matrix, *parts],
        [
            smem(),
            smem(),
            each(0, *full),
            each(0, *edge),
            each(0, *edge),
            each(first, *matrix.shape[1:]),
        ]
        + [pl.BlockSpec((rows, CHUNK, LANES), lambda i: (first, 0, 0))] * RING,
        after,
        grid=(count,),
        out_specs=[each(0, *full), each(0, *edge), each(0, *edge)],
        out_shape=[shape_of(count, *full), shape_of(count, *edge), shape_of(count, *edge)],
        scratch_shapes=[
            pltpu.VMEM((rows + 2 * HALF, CHUNK, RING * LANES), BF16),
            pltpu.VMEM(full, BF16),
        ],
    )


def rows_back_body(own_ref, low_ref, high_ref, matrix_ref, back_ref, down_ref, up_ref, x_ref):
    rows = own_ref.shape[1]
    joined_rows(x_ref, low_ref, own_ref, high_ref)
    for group in range(rows // ROW_GROUP):
        at = group * ROW_GROUP
        result = row_sums(x_ref, matrix_ref, group).astype(BF16)
        back_ref[0, at : at + ROW_GROUP] = result
        down_ref[0, at : at + ROW_GROUP] = result[:, :, : 5 * LANES]
        up_ref[0, at : at + ROW_GROUP] = result[:, :, (RING - 1) * LANES :]


def rows_back(first, own, low, high, matrix, after):
    count, rows = own.shape[:2]
    full, edge = (rows, CHUNK, RING * LANES), (HALF, CHUNK, RING * LANES)
    outs = [full, (rows, CHUNK, 5 * LANES), (rows, CHUNK, LANES)]
    return launch(
        rows_back_body,
        [own, low, high, matrix],
        [
            each(0, *full),
            each(0, *edge),
            each(0, *edge),
            each(first, *matrix.shape[1:]),
        ],
        after,
        grid=(count,),
        out_specs=[each(0, *dims) for dims in outs],
        out_shape=[shape_of(count, *dims) for dims in outs],
        scratch_shapes=[pltpu.VMEM((rows + 2 * HALF, CHUNK, RING * LANES), BF16)],
    )


def collect_body(place_ref, offset_ref, own_ref, above_ref, below_ref, matrix_ref, *refs):
    outs = refs[:RING]
    x_ref, back_ref = refs[RING:]
    rows = own_ref.shape[1]
    x_ref[:, :, :LANES] = below_ref[0]
    x_ref[:, :, LANES : 9 * LANES] = own_ref[0]
    x_ref[:, :, 9 * LANES :] = above_ref[0]
    for pair in range(6):
        at = 2 * LANES * pair
        window = x_ref[:, :, at : at + 4 * LANES].reshape(rows * CHUNK, 4 * LANES)
        result = dot_nn(window, matrix_ref[0]).astype(BF16).reshape(rows, CHUNK, 2 * LANES)
        back_ref[:, :, at : at + 2 * LANES] = result
    place = place_ref[0]

    def one_row(row, carry):
        for d in range(RING):
            slot = lax.rem(place + d, RING) + offset_ref[(RING - d) % RING, row]
            lanes = pl.ds(pl.multiple_of(slot * LANES, LANES), LANES)
            outs[d][0, row] = back_ref[row, :, lanes]
        return carry

    lax.fori_loop(0, rows, one_row, 0)


def collect(first, place, offsets, own, above, below, matrix, after):
    count, rows = own.shape[:2]
    return launch(
        collect_body,
        [place, offsets, own, above, below, matrix],
        [
            smem(),
            smem(),
            each(0, *own.shape[1:]),
            each(0, *above.shape[1:]),
            each(0, *below.shape[1:]),
            each(first, 4 * LANES, 2 * LANES),
        ],
        after,
        grid=(count,),
        out_specs=[each(0, rows, CHUNK, LANES)] * RING,
        out_shape=[shape_of(count, rows, CHUNK, LANES)] * RING,
        scratch_shapes=[
            pltpu.VMEM((rows, CHUNK, 14 * LANES), BF16),
            pltpu.VMEM((rows, CHUNK, 12 * LANES), BF16),
        ],
    )


def update_body(place_ref, index_ref, est_ref, turned_ref, col_ref, *refs):
    parts, out_ref, block_ref = refs[:RING], refs[-2], refs[-1]
    first = pl.program_id(1) * STEP
    for d in range(RING):
        at = CHUNK * lax.rem(place_ref[0] + (RING - d), RING)
        block_ref[:, pl.ds(pl.multiple_of(at, CHUNK), CHUNK)] = parts[d][0]
    for r in range(STEP):
        back = dot_nn(col_ref[0], block_ref[r]).astype(BF16)
        correction = dot_nt(turned_ref[index_ref[first + r]], back)
        out_ref[0, r] = (est_ref[0, r].astype(F32) * correction).astype(BF16)


def update(first, place, index, estimate, turned, col, parts, before):
    rows = estimate.shape[1]
    count = parts[0].shape[0]
    volume = pl.BlockSpec((1, STEP, LANES, LANES), lambda c, i: (first + c, i, 0, 0))
    in_specs = [
        smem(),
        smem(),
        volume,
        whole(turned.shape),
        pl.BlockSpec((1, LANES, LANES), lambda c, i: (first + c, 0, 0)),
    ] + [pl.BlockSpec((1, STEP, CHUNK, LANES), lambda c, i: (c, i, 0, 0))] * RING
    operands = [place, index, estimate, turned, col, *parts]
    aliases = {}
    if before is not None:
        aliases = {len(operands): 0}
        operands.append(before)
        in_specs.append(pl.BlockSpec(memory_space=pl.ANY))
    return pl.pallas_call(
        update_body,
        grid=(count, rows // STEP),
        in_specs=in_specs,
        out_specs=volume,
        out_shape=shape_of(*estimate.shape),
        scratch_shapes=[pltpu.VMEM((STEP, LANES, LANES), BF16)],
        input_output_aliases=aliases,
        compiler_params=PARAMS,
    )(*operands)


def shifted(array, axis, pairs):
    return lax.ppermute(array, axis, pairs)


HELD = 3


def per_device(estimate, observed, interp_table, psf_taps, background, block_offset, interp_index):
    channels = estimate.shape[0]
    slabs = lax.axis_size("slab")
    groups = slabs // RING
    lines = lax.axis_size("row")
    ring = [
        [(g * RING + z, g * RING + (z + d) % RING) for g in range(groups) for z in range(RING)]
        for d in range(RING)
    ]
    up = [(i, (i + RING) % slabs) for i in range(slabs)]
    down = [(i, (i - RING) % slabs) for i in range(slabs)]
    right = [(i, i + 1) for i in range(lines - 1)]
    left = [(i + 1, i) for i in range(lines - 1)]
    far_first = [4, 3, 5, 2, 6, 1, 7]

    place = lax.rem(lax.axis_index("slab"), RING).astype(jnp.int32)
    spot = place[None]
    index = interp_index[0]
    rows = estimate.shape[1]
    offset_row = jnp.pad(block_offset[0, :, 0].astype(BF16), (0, LANES - rows))
    offset_tile = jnp.broadcast_to(offset_row[None], (CHUNK, LANES))
    taps = psf_taps.reshape(3 * channels, TAPS)
    col_fwd, col_adj, eye = column_weights(spot, taps, channels)
    turned_table = jnp.swapaxes(interp_table, 1, 2)

    def spread_ring(parts):
        moved = {d: shifted(parts[d], "slab", ring[d]) for d in far_first}
        return [parts[0]] + [moved[d] for d in range(1, RING)]

    plane_fwd, plane_adj, row_fwd, row_adj = band_weights(taps, channels)
    sent = send_terms(index, estimate, interp_table, col_fwd, offset_tile)
    terms = spread_ring(sent)
    sent = send_observed(observed, eye, sent[0])
    seen = spread_ring(sent)
    ready = (sent[0],)
    offsets = jnp.stack([part[channels * rows, 0, :rows] for part in terms]).astype(jnp.int32)

    early, after = [], ready
    for c in range(channels):
        own, to_up, to_down = route(c, rows, spot, offsets, terms, after)
        from_below = shifted(to_up, "slab", up)
        from_above = shifted(to_down, "slab", down)
        passed, to_low, to_high = planes(
            c, own, to_up, from_below, from_above, plane_fwd, ()
        )
        after = (passed,) + ((seen[4], seen[3], seen[5]), (seen[2], seen[6]), ())[c]
        low = shifted(to_high, "row", right)
        high = shifted(to_low, "row", left)
        early.append((passed, low, high))

    quots, backs, sends = [], [], []
    held = {"quot": {}, "back": {}, "send": {}}

    def quotient_step(c):
        passed, low, high = early[c]
        quot, to_low, to_high = quotient(
            c, spot, background, passed, low, high, row_fwd, seen, held["quot"].get(c, ())
        )
        quots.append((quot, shifted(to_high, "row", right), shifted(to_low, "row", left)))

    def back_step(c):
        quot, low, high = quots[c]
        back, to_down, to_up = rows_back(c, quot, low, high, row_adj, held["back"].get(c, ()))
        backs.append((back, shifted(to_down, "slab", down), shifted(to_up, "slab", up)))

    def send_step(c):
        back, from_above, from_below = backs[c]
        parts = collect(
            c,
            spot,
            offsets,
            back,
            from_above,
            from_below,
            plane_adj,
            held["send"].get(c, ()),
        )
        sends.append(spread_ring(parts))

    quotient_step(0)
    quotient_step(1)
    back_step(0)
    held["quot"][2] = (backs[0][0],)
    quotient_step(2)
    back_step(1)
    send_step(0)
    held["back"][2] = (sends[0][0],)
    held["send"][1] = tuple(sends[0][d] for d in far_first[:HELD])
    back_step(2)
    send_step(1)
    held["send"][2] = tuple(sends[1][d] for d in far_first[:HELD])
    send_step(2)
    result = None
    for c in range(channels):
        result = update(c, spot, index, estimate, turned_table, col_adj, sends[c], result)
    return result


def solution(mesh):
    in_specs = (
        P(None, "row", "slab", None),
        P(None, "row", "slab", None),
        P(),
        P(),
        P(),
        P("slab", "row", None),
        P("slab", "row"),
    )
    out_specs = P(None, "row", "slab", None)
    return jax.shard_map(
        per_device, mesh=mesh, in_specs=in_specs, out_specs=out_specs, check_vma=False
    )
```

```python
import functools

import jax
import jax.numpy as jnp
from jax import lax
from jax.experimental import pallas as pl
from jax.experimental.pallas import tpu as pltpu
from jax.sharding import PartitionSpec as P

HALF = 20
TAPS = 41
RING = 8
LANES = 128
CHUNK = 16
ROW_GROUP = 16
F32 = jnp.float32
BF16 = jnp.bfloat16
PARAMS = pltpu.CompilerParams(vmem_limit_bytes=56 * 1024 * 1024)


def dot_nn(left, right):
    return lax.dot_general(left, right, (((1,), (0,)), ((), ())), preferred_element_type=F32)


def dot_nt(left, right):
    return lax.dot_general(left, right, (((1,), (1,)), ((), ())), preferred_element_type=F32)


def whole(shape):
    return pl.BlockSpec(shape, lambda *_: (0,) * len(shape))


def smem():
    return pl.BlockSpec(memory_space=pltpu.SMEM)


def shape_of(*dims):
    return jax.ShapeDtypeStruct(dims, BF16)


def launch(body, operands, in_specs, after=(), **rest):
    count = len(operands)

    def run(*refs):
        body(*refs[:count], *refs[count + len(after) :])

    return pl.pallas_call(
        run,
        in_specs=[*in_specs] + [pl.BlockSpec(memory_space=pl.ANY)] * len(after),
        compiler_params=PARAMS,
        **rest,
    )(*operands, *after)


def tap_rows(taps_ref, width, place_of):
    taps = taps_ref[...]
    kernel = (taps / jnp.sum(taps, axis=1, keepdims=True)).astype(BF16)
    tap = lax.broadcasted_iota(jnp.int32, (TAPS, width), 0)
    lane = lax.broadcasted_iota(jnp.int32, (TAPS, width), 1)
    return dot_nn(kernel, (lane == place_of(tap)).astype(BF16))


def slanted(row, height):
    spread = jnp.broadcast_to(row, (height, row.shape[1]))
    return pltpu.roll(spread, 0, 1, stride=1, stride_axis=0)


def column_weights_body(place_ref, taps_ref, fwd_ref, adj_ref, eye_ref):
    width = 2 * LANES
    fwd = tap_rows(taps_ref, width, lambda t: (t - HALF) & (width - 1))
    adj = tap_rows(taps_ref, width, lambda t: (HALF - t) & (width - 1))
    first = place_ref[0] * CHUNK
    for c in range(fwd_ref.shape[0]):
        at = 3 * c + 2
        square = slanted(fwd[at : at + 1], LANES)[:, :LANES]
        turned = pltpu.roll(square, lax.rem(LANES - first, LANES), 0)
        fwd_ref[c] = turned.astype(BF16)
        adj_ref[c] = slanted(adj[at : at + 1], LANES)[:, :LANES].astype(BF16)
    out = lax.broadcasted_iota(jnp.int32, (LANES, LANES), 0)
    taken = lax.broadcasted_iota(jnp.int32, (LANES, LANES), 1)
    eye_ref[...] = (((out + first) & (LANES - 1)) == taken).astype(BF16)


def column_weights(place, taps, channels):
    square = shape_of(channels, LANES, LANES)
    return pl.pallas_call(
        column_weights_body,
        grid=(1,),
        in_specs=[smem(), whole(taps.shape)],
        out_specs=[whole(square.shape), whole(square.shape), whole((LANES, LANES))],
        out_shape=[square, square, shape_of(LANES, LANES)],
        compiler_params=PARAMS,
    )(place, taps)


PLANE_WIDTH = 6 * LANES
ROW_WIDTH = 9 * LANES
WINDOW = (ROW_GROUP + 2 * HALF) * CHUNK


def band_weights_body(taps_ref, plane_fwd_ref, plane_adj_ref, row_fwd_ref, row_adj_ref):
    start = PLANE_WIDTH - LANES - HALF
    plane_fwd = tap_rows(taps_ref, PLANE_WIDTH, lambda t: start + 2 * HALF - t)
    plane_adj = tap_rows(taps_ref, PLANE_WIDTH, lambda t: start + t)
    row_fwd = tap_rows(taps_ref, ROW_WIDTH, lambda t: CHUNK * t)
    row_adj = tap_rows(taps_ref, ROW_WIDTH, lambda t: CHUNK * (2 * HALF - t))
    for c in range(plane_fwd_ref.shape[0]):
        plane, row = slice(3 * c, 3 * c + 1), slice(3 * c + 1, 3 * c + 2)
        for ref, band in ((plane_fwd_ref, plane_fwd), (plane_adj_ref, plane_adj)):
            ref[c] = slanted(band[plane], 4 * LANES)[:, : 2 * LANES].astype(BF16)
        for ref, band in ((row_fwd_ref, row_fwd), (row_adj_ref, row_adj)):
            ref[c] = slanted(band[row], ROW_GROUP * CHUNK)[:, :WINDOW].astype(BF16)


def band_weights(taps, channels):
    plane = shape_of(channels, 4 * LANES, 2 * LANES)
    row = shape_of(channels, ROW_GROUP * CHUNK, WINDOW)
    return pl.pallas_call(
        band_weights_body,
        grid=(1,),
        in_specs=[whole(taps.shape)],
        out_specs=[whole(v.shape) for v in (plane, plane, row, row)],
        out_shape=[plane, plane, row, row],
        compiler_params=PARAMS,
    )(taps)


STEP = 8


def send_terms_body(index_ref, est_ref, table_ref, col_ref, offset_ref, *outs):
    step = pl.program_id(0)
    blocks = pl.num_programs(0) - 1
    per_channel = LANES // CHUNK * 4 // STEP

    @pl.when(step < blocks)
    def _():
        first = lax.rem(step, per_channel) * STEP
        terms = [
            dot_nn(table_ref[index_ref[first + r]], est_ref[0, r]).astype(BF16)
            for r in range(STEP)
        ]
        turned = dot_nt(col_ref[0], jnp.concatenate(terms, axis=0)).astype(BF16)
        for r in range(STEP):
            for d in range(RING):
                outs[d][r] = turned[d * CHUNK : (d + 1) * CHUNK, r * LANES : (r + 1) * LANES]

    @pl.when(step == blocks)
    def _():
        for d in range(RING):
            outs[d][0] = offset_ref[...]


def send_terms(index, estimate, table, col, offset_tile):
    channels, rows = estimate.shape[:2]
    per_channel = rows // STEP
    blocks = channels * per_channel
    size = channels * rows + 1

    def at(i):
        j = jnp.minimum(i, blocks - 1)
        return j // per_channel, j % per_channel

    return pl.pallas_call(
        send_terms_body,
        grid=(blocks + 1,),
        in_specs=[
            smem(),
            pl.BlockSpec((1, STEP, LANES, LANES), lambda i: (*at(i), 0, 0)),
            whole(table.shape),
            pl.BlockSpec((1, LANES, LANES), lambda i: (at(i)[0], 0, 0)),
            whole(offset_tile.shape),
        ],
        out_specs=[pl.BlockSpec((STEP, CHUNK, LANES), lambda i: (i, 0, 0))] * RING,
        out_shape=[shape_of(size, CHUNK, LANES)] * RING,
        compiler_params=PARAMS,
    )(index, estimate, table, col, offset_tile)


def send_observed_body(obs_ref, eye_ref, after_ref, *outs):
    seen = dot_nt(eye_ref[...], obs_ref[0].reshape(STEP * LANES, LANES)).astype(BF16)
    for r in range(STEP):
        for d in range(RING):
            outs[d][r] = seen[d * CHUNK : (d + 1) * CHUNK, r * LANES : (r + 1) * LANES]


def send_observed(observed, eye, after):
    channels, rows = observed.shape[:2]
    per_channel = rows // STEP
    return pl.pallas_call(
        send_observed_body,
        grid=(channels * per_channel,),
        in_specs=[
            pl.BlockSpec(
                (1, STEP, LANES, LANES), lambda i: (i // per_channel, i % per_channel, 0, 0)
            ),
            whole(eye.shape),
            pl.BlockSpec(memory_space=pl.ANY),
        ],
        out_specs=[pl.BlockSpec((STEP, CHUNK, LANES), lambda i: (i, 0, 0))] * RING,
        out_shape=[shape_of(channels * rows, CHUNK, LANES)] * RING,
        compiler_params=PARAMS,
    )(observed, eye, after)


def route_body(place_ref, offset_ref, *refs):
    terms = refs[:RING]
    own_ref, up_ref, down_ref, total_ref = refs[RING:]
    rows = own_ref.shape[1]
    total_ref[...] = jnp.zeros(total_ref.shape, F32)
    place = place_ref[0]

    def one_row(row, carry):
        for d in range(RING):
            slot = lax.rem(place + (RING - d), RING) + offset_ref[d, row]
            lanes = pl.ds(pl.multiple_of(slot * LANES, LANES), LANES)
            total_ref[row, :, lanes] += terms[d][row].astype(F32)
        return carry

    lax.fori_loop(0, rows, one_row, 0)
    own_ref[0] = total_ref[:, :, : RING * LANES].astype(BF16)
    up_ref[0, :, :, : 4 * LANES] = total_ref[:, :, RING * LANES :].astype(BF16)
    up_ref[0, :, :, 4 * LANES :] = total_ref[:, :, (RING - 1) * LANES : RING * LANES].astype(BF16)
    down_ref[0] = total_ref[:, :, :LANES].astype(BF16)


def each(first, *dims):
    return pl.BlockSpec((1,) + dims, lambda i: (first + i,) + (0,) * len(dims))


def route(channel, rows, place, offsets, parts, after):
    outs = [(rows, CHUNK, RING * LANES), (rows, CHUNK, 5 * LANES), (rows, CHUNK, LANES)]
    return launch(
        route_body,
        [place, offsets, *parts],
        [smem(), smem()] + [pl.BlockSpec((rows, CHUNK, LANES), lambda i: (channel, 0, 0))] * RING,
        after,
        grid=(1,),
        out_specs=[each(0, *dims) for dims in outs],
        out_shape=[shape_of(1, *dims) for dims in outs],
        scratch_shapes=[pltpu.VMEM((rows, CHUNK, 12 * LANES), F32)],
    )


def planes_body(own_ref, spill_ref, up_ref, down_ref, matrix_ref, pass_ref, low_ref, high_ref, x_ref):
    rows = own_ref.shape[1]
    x_ref[:, :, :LANES] = up_ref[0, :, :, 4 * LANES :]
    x_ref[:, :, LANES : 5 * LANES] = (
        own_ref[0, :, :, : 4 * LANES].astype(F32) + up_ref[0, :, :, : 4 * LANES].astype(F32)
    ).astype(BF16)
    x_ref[:, :, 5 * LANES : 9 * LANES] = own_ref[0, :, :, 4 * LANES :]
    x_ref[:, :, 9 * LANES :] = (spill_ref[0].astype(F32) + down_ref[0].astype(F32)).astype(BF16)
    for pair in range(RING // 2):
        at = 2 * LANES * pair
        window = x_ref[:, :, at : at + 4 * LANES].reshape(rows * CHUNK, 4 * LANES)
        result = dot_nn(window, matrix_ref[0]).astype(BF16).reshape(rows, CHUNK, 2 * LANES)
        pass_ref[0, :, :, at : at + 2 * LANES] = result
        low_ref[0, :, :, at : at + 2 * LANES] = result[:HALF]
        high_ref[0, :, :, at : at + 2 * LANES] = result[rows - HALF :]


def planes(first, own, sent_up, from_below, from_above, matrix, after):
    count, rows = own.shape[:2]
    full, edge = (rows, CHUNK, RING * LANES), (HALF, CHUNK, RING * LANES)
    return launch(
        planes_body,
        [own, sent_up, from_below, from_above, matrix],
        [
            each(0, *full),
            each(0, rows, CHUNK, LANES),
            each(0, rows, CHUNK, 5 * LANES),
            each(0, rows, CHUNK, LANES),
            each(first, 4 * LANES, 2 * LANES),
        ],
        after,
        grid=(count,),
        out_specs=[each(0, *full), each(0, *edge), each(0, *edge)],
        out_shape=[shape_of(count, *full), shape_of(count, *edge), shape_of(count, *edge)],
        scratch_shapes=[pltpu.VMEM((rows, CHUNK, 10 * LANES), BF16)],
    )


def joined_rows(x_ref, low_ref, own_ref, high_ref):
    rows = own_ref.shape[1]
    x_ref[:HALF] = low_ref[0]
    x_ref[HALF : HALF + rows] = own_ref[0]
    x_ref[HALF + rows :] = high_ref[0]


def row_sums(x_ref, matrix_ref, group):
    window = x_ref[group * ROW_GROUP : (group + 1) * ROW_GROUP + 2 * HALF]
    flat = window.reshape((ROW_GROUP + 2 * HALF) * CHUNK, RING * LANES)
    return dot_nn(matrix_ref[0], flat).reshape(ROW_GROUP, CHUNK, RING * LANES)


def quotient_body(first, place_ref, level_ref, own_ref, low_ref, high_ref, matrix_ref, *refs):
    seen = refs[:RING]
    quot_ref, to_low_ref, to_high_ref, x_ref, obs_ref = refs[RING:]
    rows = own_ref.shape[1]
    joined_rows(x_ref, low_ref, own_ref, high_ref)
    for d in range(RING):
        slab = lax.rem(place_ref[0] + (RING - d), RING)
        obs_ref[:, :, pl.ds(pl.multiple_of(slab * LANES, LANES), LANES)] = seen[d][...]
    level = level_ref[first + pl.program_id(0)]
    for group in range(rows // ROW_GROUP):
        at = group * ROW_GROUP
        blurred = row_sums(x_ref, matrix_ref, group)
        quot_ref[0, at : at + ROW_GROUP] = (
            obs_ref[at : at + ROW_GROUP].astype(F32) / (blurred + level)
        ).astype(BF16)
    to_low_ref[0] = quot_ref[0, :HALF]
    to_high_ref[0] = quot_ref[0, rows - HALF :]


def quotient(first, place, level, own, low, high, matrix, parts, after):
    count, rows = own.shape[:2]
    full, edge = (rows, CHUNK, RING * LANES), (HALF, CHUNK, RING * LANES)
    return launch(
        functools.partial(quotient_body, first),
        [place, level, own, low, high, matrix, *parts],
        [
            smem(),
            smem(),
            each(0, *full),
            each(0, *edge),
            each(0, *edge),
            each(first, *matrix.shape[1:]),
        ]
        + [pl.BlockSpec((rows, CHUNK, LANES), lambda i: (first, 0, 0))] * RING,
        after,
        grid=(count,),
        out_specs=[each(0, *full), each(0, *edge), each(0, *edge)],
        out_shape=[shape_of(count, *full), shape_of(count, *edge), shape_of(count, *edge)],
        scratch_shapes=[
            pltpu.VMEM((rows + 2 * HALF, CHUNK, RING * LANES), BF16),
            pltpu.VMEM(full, BF16),
        ],
    )


def rows_back_body(own_ref, low_ref, high_ref, matrix_ref, back_ref, down_ref, up_ref, x_ref):
    rows = own_ref.shape[1]
    joined_rows(x_ref, low_ref, own_ref, high_ref)
    for group in range(rows // ROW_GROUP):
        at = group * ROW_GROUP
        result = row_sums(x_ref, matrix_ref, group).astype(BF16)
        back_ref[0, at : at + ROW_GROUP] = result
        down_ref[0, at : at + ROW_GROUP] = result[:, :, : 5 * LANES]
        up_ref[0, at : at + ROW_GROUP] = result[:, :, (RING - 1) * LANES :]


def rows_back(first, own, low, high, matrix, after):
    count, rows = own.shape[:2]
    full, edge = (rows, CHUNK, RING * LANES), (HALF, CHUNK, RING * LANES)
    outs = [full, (rows, CHUNK, 5 * LANES), (rows, CHUNK, LANES)]
    return launch(
        rows_back_body,
        [own, low, high, matrix],
        [
            each(0, *full),
            each(0, *edge),
            each(0, *edge),
            each(first, *matrix.shape[1:]),
        ],
        after,
        grid=(count,),
        out_specs=[each(0, *dims) for dims in outs],
        out_shape=[shape_of(count, *dims) for dims in outs],
        scratch_shapes=[pltpu.VMEM((rows + 2 * HALF, CHUNK, RING * LANES), BF16)],
    )


def collect_body(place_ref, offset_ref, own_ref, above_ref, below_ref, matrix_ref, *refs):
    outs = refs[:RING]
    x_ref, back_ref = refs[RING:]
    rows = own_ref.shape[1]
    x_ref[:, :, :LANES] = below_ref[0]
    x_ref[:, :, LANES : 9 * LANES] = own_ref[0]
    x_ref[:, :, 9 * LANES :] = above_ref[0]
    for pair in range(6):
        at = 2 * LANES * pair
        window = x_ref[:, :, at : at + 4 * LANES].reshape(rows * CHUNK, 4 * LANES)
        result = dot_nn(window, matrix_ref[0]).astype(BF16).reshape(rows, CHUNK, 2 * LANES)
        back_ref[:, :, at : at + 2 * LANES] = result
    place = place_ref[0]

    def one_row(row, carry):
        for d in range(RING):
            slot = lax.rem(place + d, RING) + offset_ref[(RING - d) % RING, row]
            lanes = pl.ds(pl.multiple_of(slot * LANES, LANES), LANES)
            outs[d][0, row] = back_ref[row, :, lanes]
        return carry

    lax.fori_loop(0, rows, one_row, 0)


def collect(first, place, offsets, own, above, below, matrix, after):
    count, rows = own.shape[:2]
    return launch(
        collect_body,
        [place, offsets, own, above, below, matrix],
        [
            smem(),
            smem(),
            each(0, *own.shape[1:]),
            each(0, *above.shape[1:]),
            each(0, *below.shape[1:]),
            each(first, 4 * LANES, 2 * LANES),
        ],
        after,
        grid=(count,),
        out_specs=[each(0, rows, CHUNK, LANES)] * RING,
        out_shape=[shape_of(count, rows, CHUNK, LANES)] * RING,
        scratch_shapes=[
            pltpu.VMEM((rows, CHUNK, 14 * LANES), BF16),
            pltpu.VMEM((rows, CHUNK, 12 * LANES), BF16),
        ],
    )


def update_body(place_ref, index_ref, est_ref, turned_ref, col_ref, *refs):
    parts, out_ref, block_ref = refs[:RING], refs[-2], refs[-1]
    first = pl.program_id(1) * STEP
    for d in range(RING):
        at = CHUNK * lax.rem(place_ref[0] + (RING - d), RING)
        block_ref[:, pl.ds(pl.multiple_of(at, CHUNK), CHUNK)] = parts[d][0]
    for r in range(STEP):
        back = dot_nn(col_ref[0], block_ref[r]).astype(BF16)
        correction = dot_nt(turned_ref[index_ref[first + r]], back)
        out_ref[0, r] = (est_ref[0, r].astype(F32) * correction).astype(BF16)


def update(first, place, index, estimate, turned, col, parts, before):
    rows = estimate.shape[1]
    count = parts[0].shape[0]
    volume = pl.BlockSpec((1, STEP, LANES, LANES), lambda c, i: (first + c, i, 0, 0))
    in_specs = [
        smem(),
        smem(),
        volume,
        whole(turned.shape),
        pl.BlockSpec((1, LANES, LANES), lambda c, i: (first + c, 0, 0)),
    ] + [pl.BlockSpec((1, STEP, CHUNK, LANES), lambda c, i: (c, i, 0, 0))] * RING
    operands = [place, index, estimate, turned, col, *parts]
    aliases = {}
    if before is not None:
        aliases = {len(operands): 0}
        operands.append(before)
        in_specs.append(pl.BlockSpec(memory_space=pl.ANY))
    return pl.pallas_call(
        update_body,
        grid=(count, rows // STEP),
        in_specs=in_specs,
        out_specs=volume,
        out_shape=shape_of(*estimate.shape),
        scratch_shapes=[pltpu.VMEM((STEP, LANES, LANES), BF16)],
        input_output_aliases=aliases,
        compiler_params=PARAMS,
    )(*operands)


def shifted(array, axis, pairs):
    return lax.ppermute(array, axis, pairs)


def per_device(estimate, observed, interp_table, psf_taps, background, block_offset, interp_index):
    channels = estimate.shape[0]
    slabs = lax.axis_size("slab")
    groups = slabs // RING
    lines = lax.axis_size("row")
    ring = [
        [(g * RING + z, g * RING + (z + d) % RING) for g in range(groups) for z in range(RING)]
        for d in range(RING)
    ]
    up = [(i, (i + RING) % slabs) for i in range(slabs)]
    down = [(i, (i - RING) % slabs) for i in range(slabs)]
    right = [(i, i + 1) for i in range(lines - 1)]
    left = [(i + 1, i) for i in range(lines - 1)]
    far_first = [4, 3, 5, 2, 6, 1, 7]

    place = lax.rem(lax.axis_index("slab"), RING).astype(jnp.int32)
    spot = place[None]
    index = interp_index[0]
    rows = estimate.shape[1]
    offset_row = jnp.pad(block_offset[0, :, 0].astype(BF16), (0, LANES - rows))
    offset_tile = jnp.broadcast_to(offset_row[None], (CHUNK, LANES))
    taps = psf_taps.reshape(3 * channels, TAPS)
    col_fwd, col_adj, eye = column_weights(spot, taps, channels)
    turned_table = jnp.swapaxes(interp_table, 1, 2)

    def spread_ring(parts):
        moved = {d: shifted(parts[d], "slab", ring[d]) for d in far_first}
        return [parts[0]] + [moved[d] for d in range(1, RING)]

    plane_fwd, plane_adj, row_fwd, row_adj = band_weights(taps, channels)
    sent = send_terms(index, estimate, interp_table, col_fwd, offset_tile)
    terms = spread_ring(sent)
    sent = send_observed(observed, eye, sent[0])
    seen = spread_ring(sent)
    ready = (sent[0],)
    offsets = jnp.stack([part[channels * rows, 0, :rows] for part in terms]).astype(jnp.int32)

    early, after = [], ready
    for c in range(channels):
        own, to_up, to_down = route(c, rows, spot, offsets, terms, after)
        from_below = shifted(to_up, "slab", up)
        from_above = shifted(to_down, "slab", down)
        passed, to_low, to_high = planes(
            c, own, to_up, from_below, from_above, plane_fwd, ()
        )
        after = (passed,) + (tuple(seen[d] for d in far_first[:5]), (), ())[c]
        low = shifted(to_high, "row", right)
        high = shifted(to_low, "row", left)
        early.append((passed, low, high))

    quots, backs, sends = [], [], []
    held = {"quot": {}, "back": {}, "send": {}}

    def quotient_step(c):
        passed, low, high = early[c]
        quot, to_low, to_high = quotient(
            c, spot, background, passed, low, high, row_fwd, seen, held["quot"].get(c, ())
        )
        quots.append((quot, shifted(to_high, "row", right), shifted(to_low, "row", left)))

    def back_step(c):
        quot, low, high = quots[c]
        back, to_down, to_up = rows_back(c, quot, low, high, row_adj, held["back"].get(c, ()))
        backs.append((back, shifted(to_down, "slab", down), shifted(to_up, "slab", up)))

    def send_step(c):
        back, from_above, from_below = backs[c]
        parts = collect(
            c,
            spot,
            offsets,
            back,
            from_above,
            from_below,
            plane_adj,
            held["send"].get(c, ()),
        )
        sends.append(spread_ring(parts))

    quotient_step(0)
    back_step(0)
    held["quot"][1] = (backs[0][0],)
    quotient_step(1)
    send_step(0)
    held["back"][1] = (sends[0][0],)
    back_step(1)
    held["quot"][2] = (sends[0][4], sends[0][3])
    quotient_step(2)
    held["send"][1] = (sends[0][5], sends[0][2])
    send_step(1)
    held["back"][2] = (sends[1][0],)
    back_step(2)
    held["send"][2] = (sends[1][4], sends[1][3], sends[1][5])
    send_step(2)
    result = None
    for c in range(channels):
        result = update(c, spot, index, estimate, turned_table, col_adj, sends[c], result)
    return result


def solution(mesh):
    in_specs = (
        P(None, "row", "slab", None),
        P(None, "row", "slab", None),
        P(),
        P(),
        P(),
        P("slab", "row", None),
        P("slab", "row"),
    )
    out_specs = P(None, "row", "slab", None)
    return jax.shard_map(
        per_device, mesh=mesh, in_specs=in_specs, out_specs=out_specs, check_vma=False
    )
```

```python
import functools

import jax
import jax.numpy as jnp
from jax import lax
from jax.experimental import pallas as pl
from jax.experimental.pallas import tpu as pltpu
from jax.sharding import PartitionSpec as P

HALF = 20
TAPS = 41
RING = 8
LANES = 128
CHUNK = 16
ROW_GROUP = 16
F32 = jnp.float32
BF16 = jnp.bfloat16
PARAMS = pltpu.CompilerParams(vmem_limit_bytes=56 * 1024 * 1024)


def dot_nn(left, right):
    return lax.dot_general(left, right, (((1,), (0,)), ((), ())), preferred_element_type=F32)


def dot_nt(left, right):
    return lax.dot_general(left, right, (((1,), (1,)), ((), ())), preferred_element_type=F32)


def whole(shape):
    return pl.BlockSpec(shape, lambda *_: (0,) * len(shape))


def smem():
    return pl.BlockSpec(memory_space=pltpu.SMEM)


def shape_of(*dims):
    return jax.ShapeDtypeStruct(dims, BF16)


def launch(body, operands, in_specs, after=(), **rest):
    count = len(operands)

    def run(*refs):
        body(*refs[:count], *refs[count + len(after) :])

    return pl.pallas_call(
        run,
        in_specs=[*in_specs] + [pl.BlockSpec(memory_space=pl.ANY)] * len(after),
        compiler_params=PARAMS,
        **rest,
    )(*operands, *after)


def tap_rows(taps_ref, width, place_of):
    taps = taps_ref[...]
    kernel = (taps / jnp.sum(taps, axis=1, keepdims=True)).astype(BF16)
    tap = lax.broadcasted_iota(jnp.int32, (TAPS, width), 0)
    lane = lax.broadcasted_iota(jnp.int32, (TAPS, width), 1)
    return dot_nn(kernel, (lane == place_of(tap)).astype(BF16))


def slanted(row, height):
    spread = jnp.broadcast_to(row, (height, row.shape[1]))
    return pltpu.roll(spread, 0, 1, stride=1, stride_axis=0)


def column_weights_body(place_ref, taps_ref, fwd_ref, adj_ref, eye_ref):
    width = 2 * LANES
    fwd = tap_rows(taps_ref, width, lambda t: (t - HALF) & (width - 1))
    adj = tap_rows(taps_ref, width, lambda t: (HALF - t) & (width - 1))
    first = place_ref[0] * CHUNK
    for c in range(fwd_ref.shape[0]):
        at = 3 * c + 2
        square = slanted(fwd[at : at + 1], LANES)[:, :LANES]
        turned = pltpu.roll(square, lax.rem(LANES - first, LANES), 0)
        fwd_ref[c] = turned.astype(BF16)
        adj_ref[c] = slanted(adj[at : at + 1], LANES)[:, :LANES].astype(BF16)
    out = lax.broadcasted_iota(jnp.int32, (LANES, LANES), 0)
    taken = lax.broadcasted_iota(jnp.int32, (LANES, LANES), 1)
    eye_ref[...] = (((out + first) & (LANES - 1)) == taken).astype(BF16)


def column_weights(place, taps, channels):
    square = shape_of(channels, LANES, LANES)
    return pl.pallas_call(
        column_weights_body,
        grid=(1,),
        in_specs=[smem(), whole(taps.shape)],
        out_specs=[whole(square.shape), whole(square.shape), whole((LANES, LANES))],
        out_shape=[square, square, shape_of(LANES, LANES)],
        compiler_params=PARAMS,
    )(place, taps)


PLANE_WIDTH = 6 * LANES
ROW_WIDTH = 9 * LANES
WINDOW = (ROW_GROUP + 2 * HALF) * CHUNK


def band_weights_body(taps_ref, plane_fwd_ref, plane_adj_ref, row_fwd_ref, row_adj_ref):
    start = PLANE_WIDTH - LANES - HALF
    plane_fwd = tap_rows(taps_ref, PLANE_WIDTH, lambda t: start + 2 * HALF - t)
    plane_adj = tap_rows(taps_ref, PLANE_WIDTH, lambda t: start + t)
    row_fwd = tap_rows(taps_ref, ROW_WIDTH, lambda t: CHUNK * t)
    row_adj = tap_rows(taps_ref, ROW_WIDTH, lambda t: CHUNK * (2 * HALF - t))
    for c in range(plane_fwd_ref.shape[0]):
        plane, row = slice(3 * c, 3 * c + 1), slice(3 * c + 1, 3 * c + 2)
        for ref, band in ((plane_fwd_ref, plane_fwd), (plane_adj_ref, plane_adj)):
            ref[c] = slanted(band[plane], 4 * LANES)[:, : 2 * LANES].astype(BF16)
        for ref, band in ((row_fwd_ref, row_fwd), (row_adj_ref, row_adj)):
            ref[c] = slanted(band[row], ROW_GROUP * CHUNK)[:, :WINDOW].astype(BF16)


def band_weights(taps, channels):
    plane = shape_of(channels, 4 * LANES, 2 * LANES)
    row = shape_of(channels, ROW_GROUP * CHUNK, WINDOW)
    return pl.pallas_call(
        band_weights_body,
        grid=(1,),
        in_specs=[whole(taps.shape)],
        out_specs=[whole(v.shape) for v in (plane, plane, row, row)],
        out_shape=[plane, plane, row, row],
        compiler_params=PARAMS,
    )(taps)


STEP = 8


def send_terms_body(index_ref, est_ref, table_ref, col_ref, offset_ref, *outs):
    step = pl.program_id(0)
    blocks = pl.num_programs(0) - 1
    per_channel = LANES // CHUNK * 4 // STEP

    @pl.when(step < blocks)
    def _():
        first = lax.rem(step, per_channel) * STEP
        terms = [
            dot_nn(table_ref[index_ref[first + r]], est_ref[0, r]).astype(BF16)
            for r in range(STEP)
        ]
        turned = dot_nt(col_ref[0], jnp.concatenate(terms, axis=0)).astype(BF16)
        for r in range(STEP):
            for d in range(RING):
                outs[d][r] = turned[d * CHUNK : (d + 1) * CHUNK, r * LANES : (r + 1) * LANES]

    @pl.when(step == blocks)
    def _():
        for d in range(RING):
            outs[d][0] = offset_ref[...]


def send_terms(index, estimate, table, col, offset_tile):
    channels, rows = estimate.shape[:2]
    per_channel = rows // STEP
    blocks = channels * per_channel
    size = channels * rows + 1

    def at(i):
        j = jnp.minimum(i, blocks - 1)
        return j // per_channel, j % per_channel

    return pl.pallas_call(
        send_terms_body,
        grid=(blocks + 1,),
        in_specs=[
            smem(),
            pl.BlockSpec((1, STEP, LANES, LANES), lambda i: (*at(i), 0, 0)),
            whole(table.shape),
            pl.BlockSpec((1, LANES, LANES), lambda i: (at(i)[0], 0, 0)),
            whole(offset_tile.shape),
        ],
        out_specs=[pl.BlockSpec((STEP, CHUNK, LANES), lambda i: (i, 0, 0))] * RING,
        out_shape=[shape_of(size, CHUNK, LANES)] * RING,
        compiler_params=PARAMS,
    )(index, estimate, table, col, offset_tile)


def send_observed_body(obs_ref, eye_ref, after_ref, *outs):
    seen = dot_nt(eye_ref[...], obs_ref[0].reshape(STEP * LANES, LANES)).astype(BF16)
    for r in range(STEP):
        for d in range(RING):
            outs[d][r] = seen[d * CHUNK : (d + 1) * CHUNK, r * LANES : (r + 1) * LANES]


def send_observed(observed, eye, after):
    channels, rows = observed.shape[:2]
    per_channel = rows // STEP
    return pl.pallas_call(
        send_observed_body,
        grid=(channels * per_channel,),
        in_specs=[
            pl.BlockSpec(
                (1, STEP, LANES, LANES), lambda i: (i // per_channel, i % per_channel, 0, 0)
            ),
            whole(eye.shape),
            pl.BlockSpec(memory_space=pl.ANY),
        ],
        out_specs=[pl.BlockSpec((STEP, CHUNK, LANES), lambda i: (i, 0, 0))] * RING,
        out_shape=[shape_of(channels * rows, CHUNK, LANES)] * RING,
        compiler_params=PARAMS,
    )(observed, eye, after)


def route_body(place_ref, offset_ref, *refs):
    terms = refs[:RING]
    own_ref, up_ref, down_ref, total_ref = refs[RING:]
    rows = own_ref.shape[1]
    total_ref[...] = jnp.zeros(total_ref.shape, F32)
    place = place_ref[0]

    def one_row(row, carry):
        for d in range(RING):
            slot = lax.rem(place + (RING - d), RING) + offset_ref[d, row]
            lanes = pl.ds(pl.multiple_of(slot * LANES, LANES), LANES)
            total_ref[row, :, lanes] += terms[d][row].astype(F32)
        return carry

    lax.fori_loop(0, rows, one_row, 0)
    own_ref[0] = total_ref[:, :, : RING * LANES].astype(BF16)
    up_ref[0, :, :, : 4 * LANES] = total_ref[:, :, RING * LANES :].astype(BF16)
    up_ref[0, :, :, 4 * LANES :] = total_ref[:, :, (RING - 1) * LANES : RING * LANES].astype(BF16)
    down_ref[0] = total_ref[:, :, :LANES].astype(BF16)


def each(first, *dims):
    return pl.BlockSpec((1,) + dims, lambda i: (first + i,) + (0,) * len(dims))


def route(channel, rows, place, offsets, parts, after):
    outs = [(rows, CHUNK, RING * LANES), (rows, CHUNK, 5 * LANES), (rows, CHUNK, LANES)]
    return launch(
        route_body,
        [place, offsets, *parts],
        [smem(), smem()] + [pl.BlockSpec((rows, CHUNK, LANES), lambda i: (channel, 0, 0))] * RING,
        after,
        grid=(1,),
        out_specs=[each(0, *dims) for dims in outs],
        out_shape=[shape_of(1, *dims) for dims in outs],
        scratch_shapes=[pltpu.VMEM((rows, CHUNK, 12 * LANES), F32)],
    )


def planes_body(own_ref, spill_ref, up_ref, down_ref, matrix_ref, pass_ref, low_ref, high_ref, x_ref):
    rows = own_ref.shape[1]
    x_ref[:, :, :LANES] = up_ref[0, :, :, 4 * LANES :]
    x_ref[:, :, LANES : 5 * LANES] = (
        own_ref[0, :, :, : 4 * LANES].astype(F32) + up_ref[0, :, :, : 4 * LANES].astype(F32)
    ).astype(BF16)
    x_ref[:, :, 5 * LANES : 9 * LANES] = own_ref[0, :, :, 4 * LANES :]
    x_ref[:, :, 9 * LANES :] = (spill_ref[0].astype(F32) + down_ref[0].astype(F32)).astype(BF16)
    for pair in range(RING // 2):
        at = 2 * LANES * pair
        window = x_ref[:, :, at : at + 4 * LANES].reshape(rows * CHUNK, 4 * LANES)
        result = dot_nn(window, matrix_ref[0]).astype(BF16).reshape(rows, CHUNK, 2 * LANES)
        pass_ref[0, :, :, at : at + 2 * LANES] = result
        low_ref[0, :, :, at : at + 2 * LANES] = result[:HALF]
        high_ref[0, :, :, at : at + 2 * LANES] = result[rows - HALF :]


def planes(first, own, sent_up, from_below, from_above, matrix, after):
    count, rows = own.shape[:2]
    full, edge = (rows, CHUNK, RING * LANES), (HALF, CHUNK, RING * LANES)
    return launch(
        planes_body,
        [own, sent_up, from_below, from_above, matrix],
        [
            each(0, *full),
            each(0, rows, CHUNK, LANES),
            each(0, rows, CHUNK, 5 * LANES),
            each(0, rows, CHUNK, LANES),
            each(first, 4 * LANES, 2 * LANES),
        ],
        after,
        grid=(count,),
        out_specs=[each(0, *full), each(0, *edge), each(0, *edge)],
        out_shape=[shape_of(count, *full), shape_of(count, *edge), shape_of(count, *edge)],
        scratch_shapes=[pltpu.VMEM((rows, CHUNK, 10 * LANES), BF16)],
    )


def joined_rows(x_ref, low_ref, own_ref, high_ref):
    rows = own_ref.shape[1]
    x_ref[:HALF] = low_ref[0]
    x_ref[HALF : HALF + rows] = own_ref[0]
    x_ref[HALF + rows :] = high_ref[0]


def row_sums(x_ref, matrix_ref, group):
    window = x_ref[group * ROW_GROUP : (group + 1) * ROW_GROUP + 2 * HALF]
    flat = window.reshape((ROW_GROUP + 2 * HALF) * CHUNK, RING * LANES)
    return dot_nn(matrix_ref[0], flat).reshape(ROW_GROUP, CHUNK, RING * LANES)


def quotient_body(first, place_ref, level_ref, own_ref, low_ref, high_ref, matrix_ref, *refs):
    seen = refs[:RING]
    quot_ref, to_low_ref, to_high_ref, x_ref, obs_ref = refs[RING:]
    rows = own_ref.shape[1]
    joined_rows(x_ref, low_ref, own_ref, high_ref)
    for d in range(RING):
        slab = lax.rem(place_ref[0] + (RING - d), RING)
        obs_ref[:, :, pl.ds(pl.multiple_of(slab * LANES, LANES), LANES)] = seen[d][...]
    level = level_ref[first + pl.program_id(0)]
    for group in range(rows // ROW_GROUP):
        at = group * ROW_GROUP
        blurred = row_sums(x_ref, matrix_ref, group)
        quot_ref[0, at : at + ROW_GROUP] = (
            obs_ref[at : at + ROW_GROUP].astype(F32) / (blurred + level)
        ).astype(BF16)
    to_low_ref[0] = quot_ref[0, :HALF]
    to_high_ref[0] = quot_ref[0, rows - HALF :]


def quotient(first, place, level, own, low, high, matrix, parts, after):
    count, rows = own.shape[:2]
    full, edge = (rows, CHUNK, RING * LANES), (HALF, CHUNK, RING * LANES)
    return launch(
        functools.partial(quotient_body, first),
        [place, level, own, low, high, matrix, *parts],
        [
            smem(),
            smem(),
            each(0, *full),
            each(0, *edge),
            each(0, *edge),
            each(first, *matrix.shape[1:]),
        ]
        + [pl.BlockSpec((rows, CHUNK, LANES), lambda i: (first, 0, 0))] * RING,
        after,
        grid=(count,),
        out_specs=[each(0, *full), each(0, *edge), each(0, *edge)],
        out_shape=[shape_of(count, *full), shape_of(count, *edge), shape_of(count, *edge)],
        scratch_shapes=[
            pltpu.VMEM((rows + 2 * HALF, CHUNK, RING * LANES), BF16),
            pltpu.VMEM(full, BF16),
        ],
    )


def rows_back_body(own_ref, low_ref, high_ref, matrix_ref, back_ref, down_ref, up_ref, x_ref):
    rows = own_ref.shape[1]
    joined_rows(x_ref, low_ref, own_ref, high_ref)
    for group in range(rows // ROW_GROUP):
        at = group * ROW_GROUP
        result = row_sums(x_ref, matrix_ref, group).astype(BF16)
        back_ref[0, at : at + ROW_GROUP] = result
        down_ref[0, at : at + ROW_GROUP] = result[:, :, : 5 * LANES]
        up_ref[0, at : at + ROW_GROUP] = result[:, :, (RING - 1) * LANES :]


def rows_back(first, own, low, high, matrix, after):
    count, rows = own.shape[:2]
    full, edge = (rows, CHUNK, RING * LANES), (HALF, CHUNK, RING * LANES)
    outs = [full, (rows, CHUNK, 5 * LANES), (rows, CHUNK, LANES)]
    return launch(
        rows_back_body,
        [own, low, high, matrix],
        [
            each(0, *full),
            each(0, *edge),
            each(0, *edge),
            each(first, *matrix.shape[1:]),
        ],
        after,
        grid=(count,),
        out_specs=[each(0, *dims) for dims in outs],
        out_shape=[shape_of(count, *dims) for dims in outs],
        scratch_shapes=[pltpu.VMEM((rows + 2 * HALF, CHUNK, RING * LANES), BF16)],
    )


def collect_body(place_ref, offset_ref, own_ref, above_ref, below_ref, matrix_ref, *refs):
    outs = refs[:RING]
    x_ref, back_ref = refs[RING:]
    rows = own_ref.shape[1]
    x_ref[:, :, :LANES] = below_ref[0]
    x_ref[:, :, LANES : 9 * LANES] = own_ref[0]
    x_ref[:, :, 9 * LANES :] = above_ref[0]
    for pair in range(6):
        at = 2 * LANES * pair
        window = x_ref[:, :, at : at + 4 * LANES].reshape(rows * CHUNK, 4 * LANES)
        result = dot_nn(window, matrix_ref[0]).astype(BF16).reshape(rows, CHUNK, 2 * LANES)
        back_ref[:, :, at : at + 2 * LANES] = result
    place = place_ref[0]

    def one_row(row, carry):
        for d in range(RING):
            slot = lax.rem(place + d, RING) + offset_ref[(RING - d) % RING, row]
            lanes = pl.ds(pl.multiple_of(slot * LANES, LANES), LANES)
            outs[d][0, row] = back_ref[row, :, lanes]
        return carry

    lax.fori_loop(0, rows, one_row, 0)


def collect(first, place, offsets, own, above, below, matrix, after):
    count, rows = own.shape[:2]
    return launch(
        collect_body,
        [place, offsets, own, above, below, matrix],
        [
            smem(),
            smem(),
            each(0, *own.shape[1:]),
            each(0, *above.shape[1:]),
            each(0, *below.shape[1:]),
            each(first, 4 * LANES, 2 * LANES),
        ],
        after,
        grid=(count,),
        out_specs=[each(0, rows, CHUNK, LANES)] * RING,
        out_shape=[shape_of(count, rows, CHUNK, LANES)] * RING,
        scratch_shapes=[
            pltpu.VMEM((rows, CHUNK, 14 * LANES), BF16),
            pltpu.VMEM((rows, CHUNK, 12 * LANES), BF16),
        ],
    )


def update_body(place_ref, index_ref, est_ref, turned_ref, col_ref, *refs):
    parts, out_ref, block_ref = refs[:RING], refs[-2], refs[-1]
    first = pl.program_id(1) * STEP
    for d in range(RING):
        at = CHUNK * lax.rem(place_ref[0] + (RING - d), RING)
        block_ref[:, pl.ds(pl.multiple_of(at, CHUNK), CHUNK)] = parts[d][0]
    for r in range(STEP):
        back = dot_nn(col_ref[0], block_ref[r]).astype(BF16)
        correction = dot_nt(turned_ref[index_ref[first + r]], back)
        out_ref[0, r] = (est_ref[0, r].astype(F32) * correction).astype(BF16)


def update(first, place, index, estimate, turned, col, parts, before):
    rows = estimate.shape[1]
    count = parts[0].shape[0]
    volume = pl.BlockSpec((1, STEP, LANES, LANES), lambda c, i: (first + c, i, 0, 0))
    in_specs = [
        smem(),
        smem(),
        volume,
        whole(turned.shape),
        pl.BlockSpec((1, LANES, LANES), lambda c, i: (first + c, 0, 0)),
    ] + [pl.BlockSpec((1, STEP, CHUNK, LANES), lambda c, i: (c, i, 0, 0))] * RING
    operands = [place, index, estimate, turned, col, *parts]
    aliases = {}
    if before is not None:
        aliases = {len(operands): 0}
        operands.append(before)
        in_specs.append(pl.BlockSpec(memory_space=pl.ANY))
    return pl.pallas_call(
        update_body,
        grid=(count, rows // STEP),
        in_specs=in_specs,
        out_specs=volume,
        out_shape=shape_of(*estimate.shape),
        scratch_shapes=[pltpu.VMEM((STEP, LANES, LANES), BF16)],
        input_output_aliases=aliases,
        compiler_params=PARAMS,
    )(*operands)


def shifted(array, axis, pairs):
    return lax.ppermute(array, axis, pairs)


def per_device(estimate, observed, interp_table, psf_taps, background, block_offset, interp_index):
    channels = estimate.shape[0]
    slabs = lax.axis_size("slab")
    groups = slabs // RING
    lines = lax.axis_size("row")
    ring = [
        [(g * RING + z, g * RING + (z + d) % RING) for g in range(groups) for z in range(RING)]
        for d in range(RING)
    ]
    up = [(i, (i + RING) % slabs) for i in range(slabs)]
    down = [(i, (i - RING) % slabs) for i in range(slabs)]
    right = [(i, i + 1) for i in range(lines - 1)]
    left = [(i + 1, i) for i in range(lines - 1)]
    far_first = [4, 3, 5, 2, 6, 1, 7]

    place = lax.rem(lax.axis_index("slab"), RING).astype(jnp.int32)
    spot = place[None]
    index = interp_index[0]
    rows = estimate.shape[1]
    offset_row = jnp.pad(block_offset[0, :, 0].astype(BF16), (0, LANES - rows))
    offset_tile = jnp.broadcast_to(offset_row[None], (CHUNK, LANES))
    taps = psf_taps.reshape(3 * channels, TAPS)
    col_fwd, col_adj, eye = column_weights(spot, taps, channels)
    turned_table = jnp.swapaxes(interp_table, 1, 2)

    def spread_ring(parts):
        moved = {d: shifted(parts[d], "slab", ring[d]) for d in far_first}
        return [parts[0]] + [moved[d] for d in range(1, RING)]

    plane_fwd, plane_adj, row_fwd, row_adj = band_weights(taps, channels)
    sent = send_terms(index, estimate, interp_table, col_fwd, offset_tile)
    terms = spread_ring(sent)
    sent = send_observed(observed, eye, sent[0])
    seen = spread_ring(sent)
    ready = (sent[0],)
    offsets = jnp.stack([part[channels * rows, 0, :rows] for part in terms]).astype(jnp.int32)

    early, after = [], ready
    for c in range(channels):
        own, to_up, to_down = route(c, rows, spot, offsets, terms, after)
        from_below = shifted(to_up, "slab", up)
        from_above = shifted(to_down, "slab", down)
        passed, to_low, to_high = planes(
            c, own, to_up, from_below, from_above, plane_fwd, ()
        )
        after = (passed,) + (tuple(seen[d] for d in far_first[:5]), (), ())[c]
        low = shifted(to_high, "row", right)
        high = shifted(to_low, "row", left)
        early.append((passed, low, high))

    quots, backs, sends = [], [], []
    held = {"quot": {}, "back": {}, "send": {}}

    def quotient_step(c):
        passed, low, high = early[c]
        quot, to_low, to_high = quotient(
            c, spot, background, passed, low, high, row_fwd, seen, held["quot"].get(c, ())
        )
        quots.append((quot, shifted(to_high, "row", right), shifted(to_low, "row", left)))

    def back_step(c):
        quot, low, high = quots[c]
        back, to_down, to_up = rows_back(c, quot, low, high, row_adj, held["back"].get(c, ()))
        backs.append((back, shifted(to_down, "slab", down), shifted(to_up, "slab", up)))

    def send_step(c):
        back, from_above, from_below = backs[c]
        parts = collect(
            c,
            spot,
            offsets,
            back,
            from_above,
            from_below,
            plane_adj,
            held["send"].get(c, ()),
        )
        sends.append(spread_ring(parts))

    quotient_step(0)
    back_step(0)
    held["quot"][1] = (backs[0][0],)
    quotient_step(1)
    send_step(0)
    held["back"][1] = (sends[0][0],)
    back_step(1)
    held["quot"][2] = (sends[0][4],)
    quotient_step(2)
    held["send"][1] = (sends[0][3],)
    send_step(1)
    held["back"][2] = (sends[1][0],)
    back_step(2)
    held["send"][2] = (sends[0][5], sends[0][2], sends[1][4])
    send_step(2)
    result = None
    for c in range(channels):
        result = update(c, spot, index, estimate, turned_table, col_adj, sends[c], result)
    return result


def solution(mesh):
    in_specs = (
        P(None, "row", "slab", None),
        P(None, "row", "slab", None),
        P(),
        P(),
        P(),
        P("slab", "row", None),
        P("slab", "row"),
    )
    out_specs = P(None, "row", "slab", None)
    return jax.shard_map(
        per_device, mesh=mesh, in_specs=in_specs, out_specs=out_specs, check_vma=False
    )
```

```python
import functools

import jax
import jax.numpy as jnp
from jax import lax
from jax.experimental import pallas as pl
from jax.experimental.pallas import tpu as pltpu
from jax.sharding import PartitionSpec as P

HALF = 20
TAPS = 41
RING = 8
LANES = 128
CHUNK = 16
ROW_GROUP = 16
F32 = jnp.float32
BF16 = jnp.bfloat16
PARAMS = pltpu.CompilerParams(vmem_limit_bytes=56 * 1024 * 1024)


def dot_nn(left, right):
    return lax.dot_general(left, right, (((1,), (0,)), ((), ())), preferred_element_type=F32)


def dot_nt(left, right):
    return lax.dot_general(left, right, (((1,), (1,)), ((), ())), preferred_element_type=F32)


def whole(shape):
    return pl.BlockSpec(shape, lambda *_: (0,) * len(shape))


def smem():
    return pl.BlockSpec(memory_space=pltpu.SMEM)


def shape_of(*dims):
    return jax.ShapeDtypeStruct(dims, BF16)


def launch(body, operands, in_specs, after=(), **rest):
    count = len(operands)

    def run(*refs):
        body(*refs[:count], *refs[count + len(after) :])

    return pl.pallas_call(
        run,
        in_specs=[*in_specs] + [pl.BlockSpec(memory_space=pl.ANY)] * len(after),
        compiler_params=PARAMS,
        **rest,
    )(*operands, *after)


def tap_rows(taps_ref, width, place_of):
    taps = taps_ref[...]
    kernel = (taps / jnp.sum(taps, axis=1, keepdims=True)).astype(BF16)
    tap = lax.broadcasted_iota(jnp.int32, (TAPS, width), 0)
    lane = lax.broadcasted_iota(jnp.int32, (TAPS, width), 1)
    return dot_nn(kernel, (lane == place_of(tap)).astype(BF16))


def slanted(row, height):
    spread = jnp.broadcast_to(row, (height, row.shape[1]))
    return pltpu.roll(spread, 0, 1, stride=1, stride_axis=0)


def column_weights_body(place_ref, taps_ref, fwd_ref, adj_ref, eye_ref):
    width = 2 * LANES
    fwd = tap_rows(taps_ref, width, lambda t: (t - HALF) & (width - 1))
    adj = tap_rows(taps_ref, width, lambda t: (HALF - t) & (width - 1))
    first = place_ref[0] * CHUNK
    for c in range(fwd_ref.shape[0]):
        at = 3 * c + 2
        square = slanted(fwd[at : at + 1], LANES)[:, :LANES]
        turned = pltpu.roll(square, lax.rem(LANES - first, LANES), 0)
        fwd_ref[c] = turned.astype(BF16)
        adj_ref[c] = slanted(adj[at : at + 1], LANES)[:, :LANES].astype(BF16)
    out = lax.broadcasted_iota(jnp.int32, (LANES, LANES), 0)
    taken = lax.broadcasted_iota(jnp.int32, (LANES, LANES), 1)
    eye_ref[...] = (((out + first) & (LANES - 1)) == taken).astype(BF16)


def column_weights(place, taps, channels):
    square = shape_of(channels, LANES, LANES)
    return pl.pallas_call(
        column_weights_body,
        grid=(1,),
        in_specs=[smem(), whole(taps.shape)],
        out_specs=[whole(square.shape), whole(square.shape), whole((LANES, LANES))],
        out_shape=[square, square, shape_of(LANES, LANES)],
        compiler_params=PARAMS,
    )(place, taps)


PLANE_WIDTH = 6 * LANES
ROW_WIDTH = 9 * LANES
WINDOW = (ROW_GROUP + 2 * HALF) * CHUNK


def band_weights_body(taps_ref, plane_fwd_ref, plane_adj_ref, row_fwd_ref, row_adj_ref):
    start = PLANE_WIDTH - LANES - HALF
    plane_fwd = tap_rows(taps_ref, PLANE_WIDTH, lambda t: start + 2 * HALF - t)
    plane_adj = tap_rows(taps_ref, PLANE_WIDTH, lambda t: start + t)
    row_fwd = tap_rows(taps_ref, ROW_WIDTH, lambda t: CHUNK * t)
    row_adj = tap_rows(taps_ref, ROW_WIDTH, lambda t: CHUNK * (2 * HALF - t))
    for c in range(plane_fwd_ref.shape[0]):
        plane, row = slice(3 * c, 3 * c + 1), slice(3 * c + 1, 3 * c + 2)
        for ref, band in ((plane_fwd_ref, plane_fwd), (plane_adj_ref, plane_adj)):
            ref[c] = slanted(band[plane], 4 * LANES)[:, : 2 * LANES].astype(BF16)
        for ref, band in ((row_fwd_ref, row_fwd), (row_adj_ref, row_adj)):
            ref[c] = slanted(band[row], ROW_GROUP * CHUNK)[:, :WINDOW].astype(BF16)


def band_weights(taps, channels):
    plane = shape_of(channels, 4 * LANES, 2 * LANES)
    row = shape_of(channels, ROW_GROUP * CHUNK, WINDOW)
    return pl.pallas_call(
        band_weights_body,
        grid=(1,),
        in_specs=[whole(taps.shape)],
        out_specs=[whole(v.shape) for v in (plane, plane, row, row)],
        out_shape=[plane, plane, row, row],
        compiler_params=PARAMS,
    )(taps)


STEP = 8


def send_terms_body(index_ref, est_ref, table_ref, col_ref, offset_ref, *outs):
    step = pl.program_id(0)
    blocks = pl.num_programs(0) - 1
    per_channel = LANES // CHUNK * 4 // STEP

    @pl.when(step < blocks)
    def _():
        first = lax.rem(step, per_channel) * STEP
        terms = [
            dot_nn(table_ref[index_ref[first + r]], est_ref[0, r]).astype(BF16)
            for r in range(STEP)
        ]
        turned = dot_nt(col_ref[0], jnp.concatenate(terms, axis=0)).astype(BF16)
        for r in range(STEP):
            for d in range(RING):
                outs[d][r] = turned[d * CHUNK : (d + 1) * CHUNK, r * LANES : (r + 1) * LANES]

    @pl.when(step == blocks)
    def _():
        for d in range(RING):
            outs[d][0] = offset_ref[...]


def send_terms(index, estimate, table, col, offset_tile):
    channels, rows = estimate.shape[:2]
    per_channel = rows // STEP
    blocks = channels * per_channel
    size = channels * rows + 1

    def at(i):
        j = jnp.minimum(i, blocks - 1)
        return j // per_channel, j % per_channel

    return pl.pallas_call(
        send_terms_body,
        grid=(blocks + 1,),
        in_specs=[
            smem(),
            pl.BlockSpec((1, STEP, LANES, LANES), lambda i: (*at(i), 0, 0)),
            whole(table.shape),
            pl.BlockSpec((1, LANES, LANES), lambda i: (at(i)[0], 0, 0)),
            whole(offset_tile.shape),
        ],
        out_specs=[pl.BlockSpec((STEP, CHUNK, LANES), lambda i: (i, 0, 0))] * RING,
        out_shape=[shape_of(size, CHUNK, LANES)] * RING,
        compiler_params=PARAMS,
    )(index, estimate, table, col, offset_tile)


def send_observed_body(obs_ref, eye_ref, after_ref, *outs):
    seen = dot_nt(eye_ref[...], obs_ref[0].reshape(STEP * LANES, LANES)).astype(BF16)
    for r in range(STEP):
        for d in range(RING):
            outs[d][r] = seen[d * CHUNK : (d + 1) * CHUNK, r * LANES : (r + 1) * LANES]


def send_observed(observed, eye, after):
    channels, rows = observed.shape[:2]
    per_channel = rows // STEP
    return pl.pallas_call(
        send_observed_body,
        grid=(channels * per_channel,),
        in_specs=[
            pl.BlockSpec(
                (1, STEP, LANES, LANES), lambda i: (i // per_channel, i % per_channel, 0, 0)
            ),
            whole(eye.shape),
            pl.BlockSpec(memory_space=pl.ANY),
        ],
        out_specs=[pl.BlockSpec((STEP, CHUNK, LANES), lambda i: (i, 0, 0))] * RING,
        out_shape=[shape_of(channels * rows, CHUNK, LANES)] * RING,
        compiler_params=PARAMS,
    )(observed, eye, after)


def route_body(place_ref, offset_ref, *refs):
    terms = refs[:RING]
    own_ref, up_ref, down_ref, total_ref = refs[RING:]
    rows = own_ref.shape[1]
    total_ref[...] = jnp.zeros(total_ref.shape, F32)
    place = place_ref[0]

    def one_row(row, carry):
        for d in range(RING):
            slot = lax.rem(place + (RING - d), RING) + offset_ref[d, row]
            lanes = pl.ds(pl.multiple_of(slot * LANES, LANES), LANES)
            total_ref[row, :, lanes] += terms[d][row].astype(F32)
        return carry

    lax.fori_loop(0, rows, one_row, 0)
    own_ref[0] = total_ref[:, :, : RING * LANES].astype(BF16)
    up_ref[0, :, :, : 4 * LANES] = total_ref[:, :, RING * LANES :].astype(BF16)
    up_ref[0, :, :, 4 * LANES :] = total_ref[:, :, (RING - 1) * LANES : RING * LANES].astype(BF16)
    down_ref[0] = total_ref[:, :, :LANES].astype(BF16)


def each(first, *dims):
    return pl.BlockSpec((1,) + dims, lambda i: (first + i,) + (0,) * len(dims))


def route(channel, rows, place, offsets, parts, after):
    outs = [(rows, CHUNK, RING * LANES), (rows, CHUNK, 5 * LANES), (rows, CHUNK, LANES)]
    return launch(
        route_body,
        [place, offsets, *parts],
        [smem(), smem()] + [pl.BlockSpec((rows, CHUNK, LANES), lambda i: (channel, 0, 0))] * RING,
        after,
        grid=(1,),
        out_specs=[each(0, *dims) for dims in outs],
        out_shape=[shape_of(1, *dims) for dims in outs],
        scratch_shapes=[pltpu.VMEM((rows, CHUNK, 12 * LANES), F32)],
    )


def planes_body(own_ref, spill_ref, up_ref, down_ref, matrix_ref, pass_ref, low_ref, high_ref, x_ref):
    rows = own_ref.shape[1]
    x_ref[:, :, :LANES] = up_ref[0, :, :, 4 * LANES :]
    x_ref[:, :, LANES : 5 * LANES] = (
        own_ref[0, :, :, : 4 * LANES].astype(F32) + up_ref[0, :, :, : 4 * LANES].astype(F32)
    ).astype(BF16)
    x_ref[:, :, 5 * LANES : 9 * LANES] = own_ref[0, :, :, 4 * LANES :]
    x_ref[:, :, 9 * LANES :] = (spill_ref[0].astype(F32) + down_ref[0].astype(F32)).astype(BF16)
    for pair in range(RING // 2):
        at = 2 * LANES * pair
        window = x_ref[:, :, at : at + 4 * LANES].reshape(rows * CHUNK, 4 * LANES)
        result = dot_nn(window, matrix_ref[0]).astype(BF16).reshape(rows, CHUNK, 2 * LANES)
        pass_ref[0, :, :, at : at + 2 * LANES] = result
        low_ref[0, :, :, at : at + 2 * LANES] = result[:HALF]
        high_ref[0, :, :, at : at + 2 * LANES] = result[rows - HALF :]


def planes(first, own, sent_up, from_below, from_above, matrix, after):
    count, rows = own.shape[:2]
    full, edge = (rows, CHUNK, RING * LANES), (HALF, CHUNK, RING * LANES)
    return launch(
        planes_body,
        [own, sent_up, from_below, from_above, matrix],
        [
            each(0, *full),
            each(0, rows, CHUNK, LANES),
            each(0, rows, CHUNK, 5 * LANES),
            each(0, rows, CHUNK, LANES),
            each(first, 4 * LANES, 2 * LANES),
        ],
        after,
        grid=(count,),
        out_specs=[each(0, *full), each(0, *edge), each(0, *edge)],
        out_shape=[shape_of(count, *full), shape_of(count, *edge), shape_of(count, *edge)],
        scratch_shapes=[pltpu.VMEM((rows, CHUNK, 10 * LANES), BF16)],
    )


def joined_rows(x_ref, low_ref, own_ref, high_ref):
    rows = own_ref.shape[1]
    x_ref[:HALF] = low_ref[0]
    x_ref[HALF : HALF + rows] = own_ref[0]
    x_ref[HALF + rows :] = high_ref[0]


def row_sums(x_ref, matrix_ref, group):
    window = x_ref[group * ROW_GROUP : (group + 1) * ROW_GROUP + 2 * HALF]
    flat = window.reshape((ROW_GROUP + 2 * HALF) * CHUNK, RING * LANES)
    return dot_nn(matrix_ref[0], flat).reshape(ROW_GROUP, CHUNK, RING * LANES)


def quotient_body(first, place_ref, level_ref, own_ref, low_ref, high_ref, matrix_ref, *refs):
    seen = refs[:RING]
    quot_ref, to_low_ref, to_high_ref, x_ref, obs_ref = refs[RING:]
    rows = own_ref.shape[1]
    joined_rows(x_ref, low_ref, own_ref, high_ref)
    for d in range(RING):
        slab = lax.rem(place_ref[0] + (RING - d), RING)
        obs_ref[:, :, pl.ds(pl.multiple_of(slab * LANES, LANES), LANES)] = seen[d][...]
    level = level_ref[first + pl.program_id(0)]
    for group in range(rows // ROW_GROUP):
        at = group * ROW_GROUP
        blurred = row_sums(x_ref, matrix_ref, group)
        quot_ref[0, at : at + ROW_GROUP] = (
            obs_ref[at : at + ROW_GROUP].astype(F32) / (blurred + level)
        ).astype(BF16)
    to_low_ref[0] = quot_ref[0, :HALF]
    to_high_ref[0] = quot_ref[0, rows - HALF :]


def quotient(first, place, level, own, low, high, matrix, parts, after):
    count, rows = own.shape[:2]
    full, edge = (rows, CHUNK, RING * LANES), (HALF, CHUNK, RING * LANES)
    return launch(
        functools.partial(quotient_body, first),
        [place, level, own, low, high, matrix, *parts],
        [
            smem(),
            smem(),
            each(0, *full),
            each(0, *edge),
            each(0, *edge),
            each(first, *matrix.shape[1:]),
        ]
        + [pl.BlockSpec((rows, CHUNK, LANES), lambda i: (first, 0, 0))] * RING,
        after,
        grid=(count,),
        out_specs=[each(0, *full), each(0, *edge), each(0, *edge)],
        out_shape=[shape_of(count, *full), shape_of(count, *edge), shape_of(count, *edge)],
        scratch_shapes=[
            pltpu.VMEM((rows + 2 * HALF, CHUNK, RING * LANES), BF16),
            pltpu.VMEM(full, BF16),
        ],
    )


def rows_back_body(own_ref, low_ref, high_ref, matrix_ref, back_ref, down_ref, up_ref, x_ref):
    rows = own_ref.shape[1]
    joined_rows(x_ref, low_ref, own_ref, high_ref)
    for group in range(rows // ROW_GROUP):
        at = group * ROW_GROUP
        result = row_sums(x_ref, matrix_ref, group).astype(BF16)
        back_ref[0, at : at + ROW_GROUP] = result
        down_ref[0, at : at + ROW_GROUP] = result[:, :, : 5 * LANES]
        up_ref[0, at : at + ROW_GROUP] = result[:, :, (RING - 1) * LANES :]


def rows_back(first, own, low, high, matrix, after):
    count, rows = own.shape[:2]
    full, edge = (rows, CHUNK, RING * LANES), (HALF, CHUNK, RING * LANES)
    outs = [full, (rows, CHUNK, 5 * LANES), (rows, CHUNK, LANES)]
    return launch(
        rows_back_body,
        [own, low, high, matrix],
        [
            each(0, *full),
            each(0, *edge),
            each(0, *edge),
            each(first, *matrix.shape[1:]),
        ],
        after,
        grid=(count,),
        out_specs=[each(0, *dims) for dims in outs],
        out_shape=[shape_of(count, *dims) for dims in outs],
        scratch_shapes=[pltpu.VMEM((rows + 2 * HALF, CHUNK, RING * LANES), BF16)],
    )


def collect_body(place_ref, offset_ref, own_ref, above_ref, below_ref, matrix_ref, *refs):
    outs = refs[:RING]
    x_ref, back_ref = refs[RING:]
    rows = own_ref.shape[1]
    x_ref[:, :, :LANES] = below_ref[0]
    x_ref[:, :, LANES : 9 * LANES] = own_ref[0]
    x_ref[:, :, 9 * LANES :] = above_ref[0]
    for pair in range(6):
        at = 2 * LANES * pair
        window = x_ref[:, :, at : at + 4 * LANES].reshape(rows * CHUNK, 4 * LANES)
        result = dot_nn(window, matrix_ref[0]).astype(BF16).reshape(rows, CHUNK, 2 * LANES)
        back_ref[:, :, at : at + 2 * LANES] = result
    place = place_ref[0]

    def one_row(row, carry):
        for d in range(RING):
            slot = lax.rem(place + d, RING) + offset_ref[(RING - d) % RING, row]
            lanes = pl.ds(pl.multiple_of(slot * LANES, LANES), LANES)
            outs[d][0, row] = back_ref[row, :, lanes]
        return carry

    lax.fori_loop(0, rows, one_row, 0)


def collect(first, place, offsets, own, above, below, matrix, after):
    count, rows = own.shape[:2]
    return launch(
        collect_body,
        [place, offsets, own, above, below, matrix],
        [
            smem(),
            smem(),
            each(0, *own.shape[1:]),
            each(0, *above.shape[1:]),
            each(0, *below.shape[1:]),
            each(first, 4 * LANES, 2 * LANES),
        ],
        after,
        grid=(count,),
        out_specs=[each(0, rows, CHUNK, LANES)] * RING,
        out_shape=[shape_of(count, rows, CHUNK, LANES)] * RING,
        scratch_shapes=[
            pltpu.VMEM((rows, CHUNK, 14 * LANES), BF16),
            pltpu.VMEM((rows, CHUNK, 12 * LANES), BF16),
        ],
    )


def update_body(place_ref, index_ref, est_ref, turned_ref, col_ref, *refs):
    parts, out_ref, block_ref = refs[:RING], refs[-2], refs[-1]
    first = pl.program_id(1) * STEP
    for d in range(RING):
        at = CHUNK * lax.rem(place_ref[0] + (RING - d), RING)
        block_ref[:, pl.ds(pl.multiple_of(at, CHUNK), CHUNK)] = parts[d][0]
    for r in range(STEP):
        back = dot_nn(col_ref[0], block_ref[r]).astype(BF16)
        correction = dot_nt(turned_ref[index_ref[first + r]], back)
        out_ref[0, r] = (est_ref[0, r].astype(F32) * correction).astype(BF16)


def update(first, place, index, estimate, turned, col, parts, before):
    rows = estimate.shape[1]
    count = parts[0].shape[0]
    volume = pl.BlockSpec((1, STEP, LANES, LANES), lambda c, i: (first + c, i, 0, 0))
    in_specs = [
        smem(),
        smem(),
        volume,
        whole(turned.shape),
        pl.BlockSpec((1, LANES, LANES), lambda c, i: (first + c, 0, 0)),
    ] + [pl.BlockSpec((1, STEP, CHUNK, LANES), lambda c, i: (c, i, 0, 0))] * RING
    operands = [place, index, estimate, turned, col, *parts]
    aliases = {}
    if before is not None:
        aliases = {len(operands): 0}
        operands.append(before)
        in_specs.append(pl.BlockSpec(memory_space=pl.ANY))
    return pl.pallas_call(
        update_body,
        grid=(count, rows // STEP),
        in_specs=in_specs,
        out_specs=volume,
        out_shape=shape_of(*estimate.shape),
        scratch_shapes=[pltpu.VMEM((STEP, LANES, LANES), BF16)],
        input_output_aliases=aliases,
        compiler_params=PARAMS,
    )(*operands)


def shifted(array, axis, pairs):
    return lax.ppermute(array, axis, pairs)


def per_device(estimate, observed, interp_table, psf_taps, background, block_offset, interp_index):
    channels = estimate.shape[0]
    slabs = lax.axis_size("slab")
    groups = slabs // RING
    lines = lax.axis_size("row")
    ring = [
        [(g * RING + z, g * RING + (z + d) % RING) for g in range(groups) for z in range(RING)]
        for d in range(RING)
    ]
    up = [(i, (i + RING) % slabs) for i in range(slabs)]
    down = [(i, (i - RING) % slabs) for i in range(slabs)]
    right = [(i, i + 1) for i in range(lines - 1)]
    left = [(i + 1, i) for i in range(lines - 1)]
    far_first = [4, 3, 5, 2, 6, 1, 7]

    place = lax.rem(lax.axis_index("slab"), RING).astype(jnp.int32)
    spot = place[None]
    index = interp_index[0]
    rows = estimate.shape[1]
    offset_row = jnp.pad(block_offset[0, :, 0].astype(BF16), (0, LANES - rows))
    offset_tile = jnp.broadcast_to(offset_row[None], (CHUNK, LANES))
    taps = psf_taps.reshape(3 * channels, TAPS)
    col_fwd, col_adj, eye = column_weights(spot, taps, channels)
    turned_table = jnp.swapaxes(interp_table, 1, 2)

    def spread_ring(parts):
        moved = {d: shifted(parts[d], "slab", ring[d]) for d in far_first}
        return [parts[0]] + [moved[d] for d in range(1, RING)]

    plane_fwd, plane_adj, row_fwd, row_adj = band_weights(taps, channels)
    sent = send_terms(index, estimate, interp_table, col_fwd, offset_tile)
    terms = spread_ring(sent)
    sent = send_observed(observed, eye, sent[0])
    seen = spread_ring(sent)
    ready = (sent[0],)
    offsets = jnp.stack([part[channels * rows, 0, :rows] for part in terms]).astype(jnp.int32)

    early, after = [], ready
    for c in range(channels):
        own, to_up, to_down = route(c, rows, spot, offsets, terms, after)
        from_below = shifted(to_up, "slab", up)
        from_above = shifted(to_down, "slab", down)
        passed, to_low, to_high = planes(
            c, own, to_up, from_below, from_above, plane_fwd, ()
        )
        after = (passed,) + (tuple(seen[d] for d in far_first[:5]), (), ())[c]
        low = shifted(to_high, "row", right)
        high = shifted(to_low, "row", left)
        early.append((passed, low, high))

    quots, backs, sends = [], [], []
    held = {"quot": {}, "back": {}, "send": {}}

    def quotient_step(c):
        passed, low, high = early[c]
        quot, to_low, to_high = quotient(
            c, spot, background, passed, low, high, row_fwd, seen, held["quot"].get(c, ())
        )
        quots.append((quot, shifted(to_high, "row", right), shifted(to_low, "row", left)))

    def back_step(c):
        quot, low, high = quots[c]
        back, to_down, to_up = rows_back(c, quot, low, high, row_adj, held["back"].get(c, ()))
        backs.append((back, shifted(to_down, "slab", down), shifted(to_up, "slab", up)))

    def send_step(c):
        back, from_above, from_below = backs[c]
        parts = collect(
            c,
            spot,
            offsets,
            back,
            from_above,
            from_below,
            plane_adj,
            held["send"].get(c, ()),
        )
        sends.append(spread_ring(parts))

    quotient_step(0)
    back_step(0)
    held["quot"][1] = (backs[0][0],)
    quotient_step(1)
    send_step(0)
    held["back"][1] = (sends[0][0],)
    back_step(1)
    held["quot"][2] = (sends[0][0],)
    quotient_step(2)
    held["send"][1] = (sends[0][4], sends[0][3])
    send_step(1)
    held["back"][2] = (sends[1][0],)
    back_step(2)
    held["send"][2] = (sends[0][5], sends[0][2], sends[1][4])
    send_step(2)
    result = None
    for c in range(channels):
        result = update(c, spot, index, estimate, turned_table, col_adj, sends[c], result)
    return result


def solution(mesh):
    in_specs = (
        P(None, "row", "slab", None),
        P(None, "row", "slab", None),
        P(),
        P(),
        P(),
        P("slab", "row", None),
        P("slab", "row"),
    )
    out_specs = P(None, "row", "slab", None)
    return jax.shard_map(
        per_device, mesh=mesh, in_specs=in_specs, out_specs=out_specs, check_vma=False
    )
```
